128 devices in a mesh: query: 4 (over y), cluster: 32 (over x, z, core).
Axes of the slice: x: 4, y: 4, z: 4, core: 2. Of those that a mesh axis runs over, the one named last changes fastest.
Arguments:
- queries: bfloat16 [4, 4096, 768], P('query', 'cluster'), may hold values from -6 to 6
- positives: int32 [4, 4096], P('query'), may hold values from 0 to 131071, as said below
- neg_clusters: int32 [4, 1024], P('query', 'cluster'), may hold values from 0 to 2047, as said below
- owner_map: int32 [2048], replicated, may hold values from 0 to 2047, as said below
- label_codes: bfloat16 [2048, 64, 768], P('cluster', 'query'), may hold values from -1 to 1
- label_scales: float32 [2048, 64, 6], P('cluster', 'query'), may hold values from 0.5 to 5
- label_master: float32 [2048, 64, 768], P('cluster', 'query'), may hold values from -13.2 to 13.2
- first_moment: float32 [2048, 64, 768], P('cluster', 'query'), may hold values from -1.8 to 1.8
- second_moment: float32 [2048, 64, 768], P('cluster', 'query'), may hold values from 0.05 to 1
Outputs:
- query_grad: float32 [4, 4096, 768], P('query', 'cluster')
- new_codes: bfloat16 [2048, 64, 768], P('cluster', 'query')
- new_scales: float32 [2048, 64, 6], P('cluster', 'query')
- new_master: float32 [2048, 64, 768], P('cluster', 'query')
- new_first: float32 [2048, 64, 768], P('cluster', 'query')
- new_second: float32 [2048, 64, 768], P('cluster', 'query')
The draws below stay inside these ranges and needn't reach their ends.
Inputs may be any that keep to these rules, and one draw needn't show every extreme that they name: `neg_clusters`: slots k * 32 to (k + 1) * 32 - 1 of a group are scored on index k of cluster. Among the slots of one such block, at most 2 name clusters whose owner_map value lies in one owner column (owner_map // 64), and every block has columns with exactly 2. All slots of one group name different clusters. `owner_map`: A permutation of the cluster ids. `positives`: each is c * 64 + r for a cluster c listed for the query's group and a row r.
All inputs are finite; a program needn't handle non-finite values. Where the reference program divides by a largest or mean magnitude, that divisor is 1e-20 or more.
Results may differ from the reference program's by a relative error of at most 0.011.
Values may be sent and summed in bfloat16 or wider, within the bound.
No kernel may reach another device: no remote copies, remote signals or barrier semaphores. Data moves between devices by JAX's collectives and lax.ppermute only.
A program may use at most 128 MiB of HBM per device.

```python
import math
import jax
import jax.numpy as jnp
from jax import lax

D = 768
BLK = 128
CROWS = 64
SLOTS_DEV = 32
CL_COL = 64
QG = 4096
CAP = 2
NEG = 1024
CLUSTERS = 2048
N_QUERY = 4
N_CLUSTER = 32


def draw_tables(key):
    base_key = jax.random.fold_in(key, 7)
    perm_key, cols_key, start_key = jax.random.split(base_key, 3)
    block_ids = jax.random.permutation(perm_key, CLUSTERS).astype(jnp.int32)
    owner_table = jnp.argsort(block_ids, stable=True).astype(jnp.int32)
    device_count = N_QUERY * N_CLUSTER
    col_keys = jax.random.split(cols_key, device_count)
    col_orders = jax.vmap(lambda one_key: jax.random.permutation(one_key, N_CLUSTER))(col_keys).astype(jnp.int32)
    half_slots = SLOTS_DEV // 2
    hot_count = half_slots // CAP
    rest_count = N_CLUSTER - hot_count
    slot_index = jnp.arange(SLOTS_DEV, dtype=jnp.int32)
    col_pick = jnp.where(slot_index < half_slots, slot_index // CAP, hot_count + (slot_index - half_slots) % rest_count)
    slot_rank = jnp.where(slot_index < half_slots, slot_index % CAP, (slot_index - half_slots) // rest_count)
    columns = col_orders[:, col_pick]
    col_table = jnp.arange(N_CLUSTER, dtype=jnp.int32)
    counts = jnp.sum((columns[:, :, None] == col_table[None, None, :]).astype(jnp.int32), axis=1).astype(jnp.int32)
    counts = counts.reshape(N_QUERY, N_CLUSTER, N_CLUSTER)
    before = (jnp.cumsum(counts, axis=1) - counts).astype(jnp.int32)
    before = before.reshape(device_count, N_CLUSTER)
    offsets = jax.random.randint(start_key, (N_QUERY, N_CLUSTER), 0, CL_COL, dtype=jnp.int32)
    offsets = jnp.repeat(offsets, N_CLUSTER, axis=0)
    first_local = jnp.take_along_axis(offsets + before, columns, axis=1)
    local_index = (first_local + slot_rank[None, :]) % CL_COL
    cluster_ids = block_ids[columns * CL_COL + local_index]
    return (cluster_ids.reshape(N_QUERY, NEG).astype(jnp.int32), owner_table)


def draw_neg_clusters(key, part):
    return draw_tables(key)[0]


def draw_owner_map(key, part):
    return draw_tables(key)[1]


def draw_positives(key, part):
    cluster_ids = draw_tables(key)[0]
    slot_key, row_key = jax.random.split(jax.random.fold_in(key, 11), 2)
    slot_pick = jax.random.randint(slot_key, (N_QUERY, QG), 0, NEG, dtype=jnp.int32)
    row_pick = jax.random.randint(row_key, (N_QUERY, QG), 0, CROWS, dtype=jnp.int32)
    chosen = jnp.take_along_axis(cluster_ids, slot_pick, axis=1)
    return (chosen * CROWS + row_pick).astype(jnp.int32)


def draw_label_master(key, part):
    value_key, row_key, col_key = jax.random.split(jax.random.fold_in(key, 3), 3)
    full_shape = (CLUSTERS, CROWS, D)
    row_scale = jnp.exp(jax.random.uniform(row_key, (CLUSTERS, CROWS, 1), jnp.float32, 0.0, math.log(3.3)))
    col_scale = jnp.exp(jax.random.uniform(col_key, (1, 1, D), jnp.float32, 0.0, math.log(3.3)))
    values = jnp.clip(jax.random.normal(value_key, full_shape, jnp.float32), -4.0, 4.0)
    return (0.3 * values * row_scale * col_scale).astype(jnp.float32)


def block_levels(own_key, dims, pieces, smallest, top_value):
    loudness, own = 1.0, jax.random.fold_in(own_key, 6)
    for dim, shards_of in pieces:
        heights = jnp.exp(jax.random.uniform(jax.random.fold_in(own, dim), (shards_of,), jnp.float32, smallest / len(pieces), top_value / len(pieces)))
        loudness = loudness * jnp.repeat(heights, dims[dim] // shards_of).reshape([-1 if axis == dim else 1 for axis in range(len(dims))])
    return loudness


def normal_values(own_key, extent, spread, most, cuts=(), kind=jnp.bfloat16):
    entries = spread * jax.random.normal(own_key, extent, jnp.float32)
    if cuts:
        entries = entries * block_levels(own_key, extent, cuts, -0.22, 0.18)
    return jnp.clip(entries, -most, most).astype(kind)


def setup_inputs(seed: int = 0) -> dict:
    splits = jax.random.split(jax.random.key(seed), 10)
    queries = normal_values(splits[0], (N_QUERY, QG, D), 1.0, 6.0, ((0, 4), (1, 32)))
    positives = draw_positives(jax.random.fold_in(splits[9], 71), 0)
    neg_clusters = draw_neg_clusters(jax.random.fold_in(splits[9], 71), 0)
    owner_map = draw_owner_map(jax.random.fold_in(splits[9], 71), 0)
    label_codes = jnp.clip(jax.random.uniform(splits[4], (CLUSTERS, CROWS, D), jnp.float32, -1.0, 1.0) * block_levels(splits[4], (CLUSTERS, CROWS, D), ((0, 32), (1, 4)), -0.4, 0.0), -1.0, 1.0).astype(jnp.bfloat16)
    label_scales = jnp.clip(jnp.exp(math.log(5.0) - 2.3025851 * jax.random.uniform(splits[5], (CLUSTERS, CROWS, D // BLK), jnp.float32) ** block_levels(splits[5], (CLUSTERS, CROWS, D // BLK), ((0, 32), (1, 4)), -0.2, 0.2)), 0.5, 5.0)
    label_master = draw_label_master(jax.random.fold_in(splits[9], 71), 0)
    first_moment = normal_values(splits[7], (CLUSTERS, CROWS, D), 0.3, 1.8, ((0, 32), (1, 4)), jnp.float32)
    second_moment = jnp.clip(jnp.exp(math.log(1.0) - 2.9957323 * jax.random.uniform(splits[8], (CLUSTERS, CROWS, D), jnp.float32) ** block_levels(splits[8], (CLUSTERS, CROWS, D), ((0, 32), (1, 4)), -0.2, 0.2)), 0.05, 1.0)
    return {"queries": queries, "positives": positives, "neg_clusters": neg_clusters, "owner_map": owner_map, "label_codes": label_codes, "label_scales": label_scales, "label_master": label_master, "first_moment": first_moment, "second_moment": second_moment}


pos_weight = 64.0
beta_first = 0.9
beta_second = 0.95
learn_rate = 0.05
adam_eps = 1e-08
adam_step = 20.0
scale_eps = 1e-06

def dequantize(quant_codes, quant_scales):
    full_shape = quant_codes.shape
    blocks = quant_codes.astype(jnp.float32).reshape(full_shape[:-1] + (full_shape[-1] // BLK, BLK))
    return (blocks * quant_scales[..., None]).reshape(full_shape).astype(jnp.bfloat16)

def adam_requantize(grad_sum, label_master, first_moment, second_moment):
    new_first = beta_first * first_moment + (1.0 - beta_first) * grad_sum
    new_second = beta_second * second_moment + (1.0 - beta_second) * grad_sum * grad_sum
    fix_first = 1.0 - beta_first ** adam_step
    fix_second = 1.0 - beta_second ** adam_step
    new_master = label_master - learn_rate * (new_first / fix_first) / (jnp.sqrt(new_second / fix_second) + adam_eps)
    full_shape = new_master.shape
    blocks = new_master.reshape(full_shape[:-1] + (full_shape[-1] // BLK, BLK))
    new_scales = lax.optimization_barrier(jnp.max(jnp.abs(blocks), axis=-1)) + scale_eps
    new_codes = (blocks / new_scales[..., None]).reshape(full_shape).astype(jnp.bfloat16)
    return (new_codes, new_scales, new_master, new_first, new_second)

def reference(queries, positives, neg_clusters, owner_map, label_codes, label_scales, label_master, first_moment, second_moment):
    inv_root = 1.0 / math.sqrt(D)
    position = owner_map[neg_clusters]
    row_index = jnp.arange(CROWS, dtype=jnp.int32)

    def one_device(running, pair):
        grad_table, query_grads = running
        group_index = pair[0]
        column_index = pair[1]
        query_rows = queries[group_index]
        positive_ids = positives[group_index]
        slot_start = column_index * SLOTS_DEV
        slot_pos = lax.dynamic_slice_in_dim(position[group_index], slot_start, SLOTS_DEV)
        slot_ids = lax.dynamic_slice_in_dim(neg_clusters[group_index], slot_start, SLOTS_DEV)
        weights = dequantize(label_codes[slot_pos], label_scales[slot_pos]).reshape(SLOTS_DEV * CROWS, D)
        label_ids = (slot_ids[:, None] * CROWS + row_index[None, :]).reshape(-1)
        scores = lax.dot_general(query_rows, weights, (((1,), (1,)), ((), ())), preferred_element_type=jnp.float32) * inv_root
        is_positive = positive_ids[:, None] == label_ids[None, :]
        slopes = jnp.where(is_positive, -pos_weight * jax.nn.sigmoid(-scores), jax.nn.sigmoid(scores)).astype(jnp.bfloat16)
        query_part = jnp.dot(slopes, weights, preferred_element_type=jnp.float32) * inv_root
        label_part = (lax.dot_general(slopes, query_rows, (((0,), (0,)), ((), ())), preferred_element_type=jnp.float32) * inv_root).astype(jnp.bfloat16)
        grad_table = grad_table.at[slot_pos].add(label_part.reshape(SLOTS_DEV, CROWS, D).astype(jnp.float32))
        query_grads = query_grads.at[group_index].add(query_part)
        return ((grad_table, query_grads), None)
    group_list = jnp.repeat(jnp.arange(N_QUERY, dtype=jnp.int32), N_CLUSTER)
    column_list = jnp.tile(jnp.arange(N_CLUSTER, dtype=jnp.int32), N_QUERY)
    start_state = (jnp.zeros((CLUSTERS, CROWS, D), jnp.float32), jnp.zeros((N_QUERY, QG, D), jnp.float32))
    final_state, unused = lax.scan(one_device, start_state, (group_list, column_list))
    grad_table, query_grads = final_state
    new_codes, new_scales, new_master, new_first, new_second = adam_requantize(grad_table, label_master, first_moment, second_moment)
    return (query_grads, new_codes, new_scales, new_master, new_first, new_second)
```

```python
import functools
import math

import jax
import jax.numpy as jnp
from jax import lax
from jax.experimental import pallas as pl
from jax.experimental.pallas import tpu as pltpu
from jax.sharding import PartitionSpec as P

BLK = 128

pos_weight = 64.0
beta_first = 0.9
beta_second = 0.95
learn_rate = 0.05
adam_eps = 1e-08
adam_step = 20.0
scale_eps = 1e-06

STEP = 4
ROWS = 512

F32, BF16, I32 = jnp.float32, jnp.bfloat16, jnp.int32
ANY = pl.BlockSpec(memory_space=pl.ANY)
VMEM_LIMIT = 62 * 1024 * 1024


def dequant_kernel(codes_ref, scales_ref, rows_ref):
    rows, width = codes_ref.shape
    for blk in range(width // BLK):
        cols = slice(blk * BLK, (blk + 1) * BLK)
        scale = jnp.broadcast_to(scales_ref[:, blk : blk + 1], (rows, BLK))
        rows_ref[:, cols] = (codes_ref[:, cols].astype(F32) * scale).astype(BF16)


def dequantize(codes, scales):
    rows, width = codes.shape
    tile = min(256, rows)
    return pl.pallas_call(
        dequant_kernel,
        out_shape=jax.ShapeDtypeStruct((rows, width), BF16),
        grid=(rows // tile,),
        in_specs=[
            pl.BlockSpec((tile, width), lambda i: (i, 0)),
            pl.BlockSpec((tile, scales.shape[1]), lambda i: (i, 0)),
        ],
        out_specs=pl.BlockSpec((tile, width), lambda i: (i, 0)),
        name="dequantize",
        cost_estimate=pl.CostEstimate(
            flops=rows * width, bytes_accessed=4 * rows * width, transcendentals=0
        ),
    )(codes, scales)


def score_kernel(
    order_ref,
    base_ref,
    info_ref,
    q_hbm,
    pid_hbm,
    w0_hbm,
    w1_hbm,
    w2a_hbm,
    w2b_hbm,
    w3a_hbm,
    w3b_hbm,
    w1b_hbm,
    qg_hbm,
    lab_hbm,
    q_ref,
    qt_ref,
    pid_ref,
    w_ref,
    acc_ref,
    wb_ref,
    id_ref,
    s_ref,
    lt_ref,
    qg_ref,
    lab_ref,
    sem,
):
    total, width = q_ref.shape
    n_col, quarter = w_ref.shape[1], w_ref.shape[2]
    half = n_col // 2
    crows = 4 * quarter
    n_chunk = total // ROWS
    inv_root = 1.0 / math.sqrt(width)
    listed = info_ref[0]
    my_y = info_ref[1]
    n_block = (listed + STEP - 1) // STEP

    loads = [
        pltpu.make_async_copy(w0_hbm, w_ref.at[0], sem.at[0]),
        pltpu.make_async_copy(w1_hbm, w_ref.at[1, pl.ds(0, half)], sem.at[1]),
        pltpu.make_async_copy(w1b_hbm, w_ref.at[1, pl.ds(half, half)], sem.at[2]),
        pltpu.make_async_copy(w2a_hbm, w_ref.at[2, pl.ds(0, half)], sem.at[3]),
        pltpu.make_async_copy(w2b_hbm, w_ref.at[2, pl.ds(half, half)], sem.at[4]),
        pltpu.make_async_copy(w3a_hbm, w_ref.at[3, pl.ds(0, half)], sem.at[5]),
        pltpu.make_async_copy(w3b_hbm, w_ref.at[3, pl.ds(half, half)], sem.at[6]),
        pltpu.make_async_copy(pid_hbm, pid_ref, sem.at[7]),
    ]
    load_q = pltpu.make_async_copy(q_hbm, q_ref, sem.at[8])
    load_q.start()
    for copy in loads:
        copy.start()

    def clear(i, carry):
        rows = pl.ds(pl.multiple_of(i * 64, 64), 64)
        acc_ref[rows, :] = jnp.zeros((64, width), F32)
        return carry

    lax.fori_loop(0, total // 64, clear, 0)

    def clear_labels(i, carry):
        for j in range(4):
            lab_ref[j, i] = jnp.zeros((quarter, width), BF16)
        return carry

    lax.fori_loop(0, n_col, clear_labels, 0)

    load_q.wait()

    def flip(i, carry):
        rows = pl.ds(pl.multiple_of(i * 256, 256), 256)
        qt_ref[:, rows] = q_ref[rows, :].T
        return carry

    lax.fori_loop(0, total // 256, flip, 0)

    for copy in loads:
        copy.wait()

    lane = lax.broadcasted_iota(I32, (8, STEP * crows), 1)
    slot = lax.div(lane, jnp.full_like(lane, crows))
    within = lax.rem(lane, jnp.full_like(lane, crows))
    part = lax.rem(lax.div(within, jnp.full_like(lane, quarter)) + my_y, jnp.full_like(lane, 4))
    row_id = part * quarter + lax.rem(within, jnp.full_like(lane, quarter))

    def stage(block):
        buf = lax.rem(block, 2)
        ids = row_id
        for k in range(STEP):
            entry = jnp.minimum(block * STEP + k, n_col - 1)
            valid = block * STEP + k < listed
            where = order_ref[entry]
            ids = ids + jnp.where(slot == k, base_ref[entry], 0)
            for j in range(4):
                rows = w_ref[j, where]
                start = k * crows + j * quarter
                wb_ref[buf, start : start + quarter, :] = jnp.where(
                    valid, rows, jnp.zeros_like(rows)
                )
        id_ref[buf] = ids

    def score(block, chunk):
        rows = pl.ds(pl.multiple_of(chunk * ROWS, ROWS), ROWS)
        return lax.dot_general(
            q_ref[rows, :],
            wb_ref[lax.rem(block, 2)],
            (((1,), (1,)), ((), ())),
            preferred_element_type=F32,
        )

    def slopes_of(block, chunk, scores):
        rows = pl.ds(pl.multiple_of(chunk * ROWS, ROWS), ROWS)
        pid = pid_ref[rows, :]
        ids = id_ref[lax.rem(block, 2)]
        parts = []
        for c in range(STEP * crows // 128):
            cols = slice(c * 128, (c + 1) * 128)
            x = scores[:, cols] * inv_root
            hit = pid == ids[0:1, cols]
            prob = 1.0 / (1.0 + jnp.exp(jnp.where(hit, x, -x)))
            parts.append(jnp.where(hit, -pos_weight * prob, prob).astype(BF16))
        return jnp.concatenate(parts, axis=1)

    @pl.when(n_block > 0)
    def _():
        stage(0)
        s_ref[0] = score(0, 0)

    def step(t, carry):
        block, chunk = lax.div(t, n_chunk), lax.rem(t, n_chunk)
        nxt = t + 1
        nblock, nchunk = lax.div(nxt, n_chunk), lax.rem(nxt, n_chunk)

        @pl.when(chunk == 0)
        def _():
            lt_ref[...] = jnp.zeros_like(lt_ref)

        @pl.when(nchunk == 0)
        def _():
            stage(nblock)

        rows = pl.ds(pl.multiple_of(chunk * ROWS, ROWS), ROWS)
        s_ref[lax.rem(nxt, 2)] = score(nblock, nchunk)
        p = slopes_of(block, chunk, s_ref[lax.rem(t, 2)])
        acc_ref[rows, :] += jnp.dot(p, wb_ref[lax.rem(block, 2)], preferred_element_type=F32)
        lt_ref[...] += jnp.dot(qt_ref[:, rows], p, preferred_element_type=F32)

        @pl.when(nchunk == 0)
        def _():
            lab = (lt_ref[...] * inv_root).T.astype(BF16)
            for k in range(STEP):
                entry = block * STEP + k

                @pl.when(entry < listed)
                def _(k=k, entry=entry):
                    where = order_ref[entry]
                    for j in range(4):
                        start = k * crows + j * quarter
                        lab_ref[j, where] = lab[start : start + quarter, :]

        return carry

    lax.fori_loop(0, n_block * n_chunk, step, 0)

    put_lab = pltpu.make_async_copy(lab_ref, lab_hbm, sem.at[9])
    put_lab.start()

    def finish(i, carry):
        rows = pl.ds(pl.multiple_of(i * 64, 64), 64)
        qg_ref[rows, :] = (acc_ref[rows, :] * inv_root).astype(BF16)
        return carry

    lax.fori_loop(0, total // 64, finish, 0)
    put_qg = pltpu.make_async_copy(qg_ref, qg_hbm, sem.at[10])
    put_qg.start()
    put_lab.wait()
    put_qg.wait()


def score_and_grads(order, base, info, queries, pid, quarters):
    total, width = queries.shape
    n_col, quarter = quarters[0].shape[0], quarters[0].shape[1]
    block = STEP * 4 * quarter
    smem = pl.BlockSpec(memory_space=pltpu.SMEM)
    return pl.pallas_call(
        score_kernel,
        out_shape=(
            jax.ShapeDtypeStruct((total, width), BF16),
            jax.ShapeDtypeStruct((4, n_col, quarter, width), BF16),
        ),
        in_specs=[smem] * 3 + [ANY] * 9,
        out_specs=(ANY, ANY),
        scratch_shapes=[
            pltpu.VMEM((total, width), BF16),
            pltpu.VMEM((width, total), BF16),
            pltpu.VMEM((total, 128), I32),
            pltpu.VMEM((4, n_col, quarter, width), BF16),
            pltpu.VMEM((total, width), F32),
            pltpu.VMEM((2, block, width), BF16),
            pltpu.VMEM((2, 8, block), I32),
            pltpu.VMEM((2, ROWS, block), F32),
            pltpu.VMEM((width, block), F32),
            pltpu.VMEM((total, width), BF16),
            pltpu.VMEM((4, n_col, quarter, width), BF16),
            pltpu.SemaphoreType.DMA((11,)),
        ],
        compiler_params=pltpu.CompilerParams(vmem_limit_bytes=VMEM_LIMIT),
        name="score",
        cost_estimate=pl.CostEstimate(
            flops=3 * total * n_col * 2 * quarter * width * 2,
            bytes_accessed=8 * total * width,
            transcendentals=total * n_col * 4 * quarter,
        ),
    )(order, base, info, queries, pid, *quarters)


def update_kernel(
    own_ref, left_ref, right_ref, master_ref, first_ref, second_ref,
    codes_ref, scales_ref, master_out, first_out, second_out,
):
    width = master_ref.shape[1]
    fix_first = 1.0 - beta_first**adam_step
    fix_second = 1.0 - beta_second**adam_step
    peaks = []
    for blk in range(width // BLK):
        cols = slice(blk * BLK, (blk + 1) * BLK)
        grad = (
            own_ref[:, cols].astype(F32)
            + left_ref[:, cols].astype(F32)
            + right_ref[:, cols].astype(F32)
        )
        first = beta_first * first_ref[:, cols] + (1.0 - beta_first) * grad
        second = beta_second * second_ref[:, cols] + (1.0 - beta_second) * grad * grad
        master = master_ref[:, cols] - learn_rate * (first / fix_first) / (
            jnp.sqrt(second / fix_second) + adam_eps
        )
        peak = jnp.max(jnp.abs(master), axis=1, keepdims=True) + scale_eps
        codes_ref[:, cols] = (master / peak).astype(BF16)
        master_out[:, cols] = master
        first_out[:, cols] = first
        second_out[:, cols] = second
        peaks.append(peak)
    scales_ref[...] = jnp.concatenate(peaks, axis=1)


def update(own, left, right, master, first, second):
    rows, width = master.shape
    tile = min(128, rows)
    spec = pl.BlockSpec((tile, width), lambda i: (i, 0))
    blocks = width // BLK
    return pl.pallas_call(
        update_kernel,
        out_shape=(
            jax.ShapeDtypeStruct((rows, width), BF16),
            jax.ShapeDtypeStruct((rows, blocks), F32),
            jax.ShapeDtypeStruct((rows, width), F32),
            jax.ShapeDtypeStruct((rows, width), F32),
            jax.ShapeDtypeStruct((rows, width), F32),
        ),
        grid=(rows // tile,),
        in_specs=[spec] * 6,
        out_specs=(spec, pl.BlockSpec((tile, blocks), lambda i: (i, 0)), spec, spec, spec),
        compiler_params=pltpu.CompilerParams(vmem_limit_bytes=32 * 1024 * 1024),
        name="update",
        cost_estimate=pl.CostEstimate(
            flops=20 * rows * width, bytes_accessed=32 * rows * width, transcendentals=rows * width
        ),
    )(own, left, right, master, first, second)


def shift(value, by):
    size = lax.axis_size("query")
    return lax.ppermute(value, "query", [(i, (i + by) % size) for i in range(size)])


def per_device(
    queries,
    positives,
    neg_clusters,
    owner_map,
    label_codes,
    label_scales,
    label_master,
    first_moment,
    second_moment,
):
    n_col, quarter, width = label_codes.shape
    crows = 4 * quarter
    half = n_col // 2
    my_y = lax.axis_index("query")
    my_col = lax.axis_index("cluster")

    own = dequantize(
        label_codes.reshape(n_col * quarter, width),
        label_scales.reshape(n_col * quarter, width // BLK),
    ).reshape(n_col, quarter, width)
    low, high = own[:half], own[half:]
    left_low = shift(low, 1)
    right_high = shift(high, -1)
    left_high = shift(high, 1)
    right_low = shift(low, -1)
    far_low = shift(left_low, 1)
    far_high = shift(right_high, -1)

    query_rows = lax.all_gather(queries, "cluster", axis=1, tiled=True)[0]
    group_ids = lax.all_gather(neg_clusters, "cluster", axis=0, tiled=True).reshape(-1)

    places = my_col * n_col + jnp.arange(n_col, dtype=I32)
    all_ids = jnp.arange(owner_map.shape[0], dtype=I32)
    held = jnp.sum(jnp.where(owner_map[None, :] == places[:, None], all_ids[None, :], 0), axis=1)
    listed = jnp.sum((group_ids[None, :] == held[:, None]).astype(I32), axis=1)
    count = jnp.sum(listed)
    local = jnp.arange(n_col, dtype=I32)
    before = local[None, :] < local[:, None]
    ahead = jnp.sum(jnp.where(before, listed[None, :], 0), axis=1)
    rank = jnp.where(listed > 0, ahead, count + local - ahead)
    place = rank[None, :] == local[:, None]
    order = jnp.sum(jnp.where(place, local[None, :], 0), axis=1)
    base = jnp.sum(jnp.where(place, held[None, :], 0), axis=1) * crows
    info = jnp.stack([count, my_y.astype(I32)])
    pid = jnp.broadcast_to(positives[0][:, None], (positives.shape[1], 128))

    query_part, label_part = score_and_grads(
        order,
        base,
        info,
        query_rows,
        pid,
        (own, right_low, far_low, far_high, left_low, left_high, right_high),
    )

    query_grad = lax.psum_scatter(
        query_part, "cluster", scatter_dimension=0, tiled=True
    ).astype(F32)

    via_left = shift(label_part[2, :half], 1)
    via_right = shift(label_part[2, half:], -1)
    left_b = shift(label_part[1, half:], 1)
    right_b = shift(label_part[3, :half], -1)
    left_a = shift(label_part[1, :half] + via_left, 1)
    right_a = shift(label_part[3, half:] + via_right, -1)
    from_left = jnp.concatenate([left_a, left_b])
    from_right = jnp.concatenate([right_b, right_a])

    flat = lambda value: value.reshape(n_col * quarter, width)
    new_codes, new_scales, new_master, new_first, new_second = update(
        flat(label_part[0]),
        flat(from_left),
        flat(from_right),
        flat(label_master),
        flat(first_moment),
        flat(second_moment),
    )
    shape = label_master.shape
    return (
        query_grad[None],
        new_codes.reshape(shape),
        new_scales.reshape(n_col, quarter, width // BLK),
        new_master.reshape(shape),
        new_first.reshape(shape),
        new_second.reshape(shape),
    )


def solution(mesh):
    in_specs = (
        P("query", "cluster", None),
        P("query", None),
        P("query", "cluster"),
        P(),
        P("cluster", "query", None),
        P("cluster", "query", None),
        P("cluster", "query", None),
        P("cluster", "query", None),
        P("cluster", "query", None),
    )
    out_specs = (
        P("query", "cluster", None),
        P("cluster", "query", None),
        P("cluster", "query", None),
        P("cluster", "query", None),
        P("cluster", "query", None),
        P("cluster", "query", None),
    )
    return jax.shard_map(
        per_device, mesh=mesh, in_specs=in_specs, out_specs=out_specs, check_vma=False
    )
```

```python
import functools
import math

import jax
import jax.numpy as jnp
from jax import lax
from jax.experimental import pallas as pl
from jax.experimental.pallas import tpu as pltpu
from jax.sharding import PartitionSpec as P

BLK = 128

pos_weight = 64.0
beta_first = 0.9
beta_second = 0.95
learn_rate = 0.05
adam_eps = 1e-08
adam_step = 20.0
scale_eps = 1e-06

STEP = 4
SUB = 512
FLIP = 512
SPLIT1, SPLIT2, SPLIT3 = 1,1,1

F32, BF16, I32 = jnp.float32, jnp.bfloat16, jnp.int32
ANY = pl.BlockSpec(memory_space=pl.ANY)
VMEM_LIMIT = 62 * 1024 * 1024


def dequant_kernel(codes_ref, scales_ref, rows_ref):
    rows, width = codes_ref.shape
    for blk in range(width // BLK):
        cols = slice(blk * BLK, (blk + 1) * BLK)
        scale = jnp.broadcast_to(scales_ref[:, blk : blk + 1], (rows, BLK))
        rows_ref[:, cols] = (codes_ref[:, cols].astype(F32) * scale).astype(BF16)


def dequantize(codes, scales):
    rows, width = codes.shape
    tile = min(256, rows)
    return pl.pallas_call(
        dequant_kernel,
        out_shape=jax.ShapeDtypeStruct((rows, width), BF16),
        grid=(rows // tile,),
        in_specs=[
            pl.BlockSpec((tile, width), lambda i: (i, 0)),
            pl.BlockSpec((tile, scales.shape[1]), lambda i: (i, 0)),
        ],
        out_specs=pl.BlockSpec((tile, width), lambda i: (i, 0)),
        name="dequantize",
        cost_estimate=pl.CostEstimate(
            flops=rows * width, bytes_accessed=4 * rows * width, transcendentals=0
        ),
    )(codes, scales)


def score_kernel(first, *refs):
    order_ref, base_ref, info_ref, q_hbm, pid_hbm = refs[:5]
    pieces = refs[5:12]
    refs = refs[12:]
    if not first:
        lab_in, refs = refs[0], refs[1:]
    qg_out, lab_out = refs[:2]
    q_ref, qt_ref, pid_ref, w_ref, acc_ref, wb_ref, id_ref, sa_ref, sb_ref = refs[2:11]
    pa_ref, pb_ref, lt_ref, lab_ref, qg_ref, sem, q_sem, out_sem = refs[11:]
    total, width = q_ref.shape
    n_col, quarter = w_ref.shape[1], w_ref.shape[2]
    half = n_col // 2
    crows = 4 * quarter
    rows = STEP * crows
    n_pair = total // (2 * SUB)
    inv_root = 1.0 / math.sqrt(width)
    power_scale = math.log2(math.e) * inv_root
    listed = info_ref[0]
    my_y = info_ref[1]
    n_block = lax.div(listed + STEP - 1, STEP)

    def rows_of(start, size):
        return pl.ds(pl.multiple_of(start, size), size)

    load_q = [
        pltpu.make_async_copy(
            q_hbm.at[pl.ds(i * FLIP, FLIP)], q_ref.at[pl.ds(i * FLIP, FLIP)], q_sem.at[i]
        )
        for i in range(total // FLIP)
    ]
    targets = [
        w_ref.at[0],
        w_ref.at[1, pl.ds(0, half)],
        w_ref.at[2, pl.ds(0, half)],
        w_ref.at[2, pl.ds(half, half)],
        w_ref.at[3, pl.ds(0, half)],
        w_ref.at[3, pl.ds(half, half)],
        w_ref.at[1, pl.ds(half, half)],
    ]
    loads = [
        pltpu.make_async_copy(src, dst, sem.at[i])
        for i, (src, dst) in enumerate(zip(pieces, targets, strict=True))
    ]
    loads.append(pltpu.make_async_copy(pid_hbm, pid_ref, sem.at[7]))
    if not first:
        loads.append(pltpu.make_async_copy(lab_in, lab_ref, sem.at[8]))
    for copy in load_q + loads:
        copy.start()

    if first:

        def clear(entry, carry):
            where = order_ref[entry]
            for j in range(4):
                lab_ref[j, where] = jnp.zeros((quarter, width), BF16)
            return carry

        lax.fori_loop(listed, n_col, clear, 0)

    for i, copy in enumerate(load_q):
        copy.wait()

        def flip(k, carry, i=i):
            at = rows_of(i * FLIP + k * 256, 256)
            qt_ref[:, at] = q_ref[at, :].T
            return carry

        lax.fori_loop(0, FLIP // 256, flip, 0)

    for copy in loads:
        copy.wait()

    lane = lax.broadcasted_iota(I32, (8, rows), 1)
    slot = lax.div(lane, jnp.full_like(lane, crows))
    within = lax.rem(lane, jnp.full_like(lane, crows))
    part = lax.rem(lax.div(within, jnp.full_like(lane, quarter)) + my_y, jnp.full_like(lane, 4))
    row_id = part * quarter + lax.rem(within, jnp.full_like(lane, quarter))

    def stage(block):
        buf = lax.rem(block, 2)
        ids = row_id
        for k in range(STEP):
            entry = jnp.minimum(block * STEP + k, n_col - 1)
            valid = block * STEP + k < listed
            where = order_ref[entry]
            ids = ids + jnp.where(slot == k, base_ref[entry], 0)
            for j in range(4):
                start = k * crows + j * quarter
                held = w_ref[j, where]
                wb_ref[buf, start : start + quarter, :] = jnp.where(
                    valid, held, jnp.zeros_like(held)
                )
        id_ref[buf] = ids

    def score(block, start, to_ref):
        size = SUB // SPLIT1
        for h in range(SPLIT1):
            to_ref[h * size : (h + 1) * size] = lax.dot_general(
                q_ref[rows_of(start + h * size, size), :],
                wb_ref[lax.rem(block, 2)],
                (((1,), (1,)), ((), ())),
                preferred_element_type=F32,
            )

    def slopes(block, start, from_ref, to_ref):
        pid = pid_ref[rows_of(start, SUB), :]
        ids = id_ref[lax.rem(block, 2)]
        for c in range(rows // 128):
            cols = slice(c * 128, (c + 1) * 128)
            hit = pid == ids[0:1, cols]
            power = from_ref[:, cols] * jnp.where(hit, power_scale, -power_scale)
            prob = jnp.where(hit, -pos_weight, 1.0) / (1.0 + jnp.exp2(power))
            to_ref[:, cols] = prob.astype(BF16)

    def grads(block, start, p_ref, lt_is_new):
        size = SUB // SPLIT2
        for h in range(SPLIT2):
            at = rows_of(start + h * size, size)
            old = jnp.where(block == 0, 0.0, acc_ref[at, :])
            acc_ref[at, :] = old + jnp.dot(
                p_ref[h * size : (h + 1) * size],
                wb_ref[lax.rem(block, 2)],
                preferred_element_type=F32,
            )
        buf = lax.rem(block, 2)
        size = width // SPLIT3
        for h in range(SPLIT3):
            cols = slice(h * size, (h + 1) * size)
            old = jnp.where(lt_is_new, 0.0, lt_ref[buf, cols])
            lt_ref[buf, cols] = old + jnp.dot(
                qt_ref[cols, rows_of(start, SUB)], p_ref[...], preferred_element_type=F32
            )

    def emit(block):
        lab = (lt_ref[lax.rem(block, 2)] * inv_root).T
        for k in range(STEP):
            entry = block * STEP + k

            @pl.when(entry < listed)
            def _(k=k, entry=entry):
                where = order_ref[entry]
                for j in range(4):
                    start = k * crows + j * quarter
                    piece = lab[start : start + quarter, :]
                    if not first:
                        piece = piece + lab_ref[j, where].astype(F32)
                    lab_ref[j, where] = piece.astype(BF16)

    @pl.when(n_block > 0)
    def _():
        stage(0)
        score(0, 0, sa_ref)
        pb_ref[...] = jnp.zeros_like(pb_ref)

    def pair(t, carry):
        block, at = lax.div(t, n_pair), lax.rem(t, n_pair)
        before = jnp.maximum(t - 1, 0)
        pblock, pat = lax.div(before, n_pair), lax.rem(before, n_pair)
        nblock, nat = lax.div(t + 1, n_pair), lax.rem(t + 1, n_pair)
        here = at * (2 * SUB)

        @pl.when(nat == 0)
        def _():
            stage(nblock)

        @pl.when((at == 1) & (block > 0))
        def _():
            emit(block - 1)

        slopes(block, here, sa_ref, pa_ref)
        score(block, here + SUB, sb_ref)
        grads(pblock, pat * (2 * SUB) + SUB, pb_ref, False)
        slopes(block, here + SUB, sb_ref, pb_ref)
        score(nblock, nat * (2 * SUB), sa_ref)
        grads(block, here, pa_ref, at == 0)
        return carry

    lax.fori_loop(0, n_block * n_pair, pair, 0)

    @pl.when(n_block > 0)
    def _():
        grads(n_block - 1, total - SUB, pb_ref, False)
        emit(n_block - 1)

    put_lab = pltpu.make_async_copy(lab_ref, lab_out, out_sem.at[0])
    put_lab.start()
    put_q = []
    for i in range(total // FLIP):

        def finish(k, carry, i=i):
            at = rows_of(i * FLIP + k * 64, 64)
            qg_ref[at, :] = jnp.where(n_block > 0, acc_ref[at, :] * inv_root, 0.0).astype(BF16)
            return carry

        lax.fori_loop(0, FLIP // 64, finish, 0)
        put_q.append(
            pltpu.make_async_copy(
                qg_ref.at[pl.ds(i * FLIP, FLIP)], qg_out.at[pl.ds(i * FLIP, FLIP)], out_sem.at[i + 1]
            )
        )
        put_q[-1].start()
    put_lab.wait()
    for copy in put_q:
        copy.wait()


def score_and_grads(order, base, info, queries, pid, quarters, earlier=None):
    total, width = queries.shape
    n_col, quarter = quarters[0].shape[0], quarters[0].shape[1]
    block = STEP * 4 * quarter
    smem = pl.BlockSpec(memory_space=pltpu.SMEM)
    first = earlier is None
    pieces = total // FLIP
    return pl.pallas_call(
        functools.partial(score_kernel, first),
        out_shape=(
            jax.ShapeDtypeStruct((total, width), BF16),
            jax.ShapeDtypeStruct((4, n_col, quarter, width), BF16),
        ),
        in_specs=[smem] * 3 + [ANY] * (9 if first else 10),
        out_specs=(ANY, ANY),
        scratch_shapes=[
            pltpu.VMEM((total, width), BF16),
            pltpu.VMEM((width, total), BF16),
            pltpu.VMEM((total, 128), I32),
            pltpu.VMEM((4, n_col, quarter, width), BF16),
            pltpu.VMEM((total, width), F32),
            pltpu.VMEM((2, block, width), BF16),
            pltpu.VMEM((2, 8, block), I32),
            pltpu.VMEM((SUB, block), F32),
            pltpu.VMEM((SUB, block), F32),
            pltpu.VMEM((SUB, block), BF16),
            pltpu.VMEM((SUB, block), BF16),
            pltpu.VMEM((2, width, block), F32),
            pltpu.VMEM((4, n_col, quarter, width), BF16),
            pltpu.VMEM((total, width), BF16),
            pltpu.SemaphoreType.DMA((9,)),
            pltpu.SemaphoreType.DMA((pieces,)),
            pltpu.SemaphoreType.DMA((pieces + 1,)),
        ],
        compiler_params=pltpu.CompilerParams(vmem_limit_bytes=VMEM_LIMIT),
        name="score" if first else "score_more",
        cost_estimate=pl.CostEstimate(
            flops=3 * total * n_col * 2 * quarter * width * 2,
            bytes_accessed=4 * total * width + 16 * n_col * quarter * width,
            transcendentals=total * n_col * 4 * quarter,
        ),
    )(order, base, info, queries, pid, *quarters, *(() if first else (earlier,)))


def update_kernel(
    own_ref, left_ref, right_ref, master_ref, first_ref, second_ref,
    codes_ref, scales_ref, master_out, first_out, second_out,
):
    width = master_ref.shape[1]
    fix_first = 1.0 - beta_first**adam_step
    fix_second = 1.0 - beta_second**adam_step
    peaks = []
    for blk in range(width // BLK):
        cols = slice(blk * BLK, (blk + 1) * BLK)
        grad = (
            own_ref[:, cols].astype(F32)
            + left_ref[:, cols].astype(F32)
            + right_ref[:, cols].astype(F32)
        )
        first = beta_first * first_ref[:, cols] + (1.0 - beta_first) * grad
        second = beta_second * second_ref[:, cols] + (1.0 - beta_second) * grad * grad
        master = master_ref[:, cols] - learn_rate * (first / fix_first) / (
            jnp.sqrt(second / fix_second) + adam_eps
        )
        peak = jnp.max(jnp.abs(master), axis=1, keepdims=True) + scale_eps
        codes_ref[:, cols] = (master / peak).astype(BF16)
        master_out[:, cols] = master
        first_out[:, cols] = first
        second_out[:, cols] = second
        peaks.append(peak)
    scales_ref[...] = jnp.concatenate(peaks, axis=1)


def update(own, left, right, master, first, second):
    rows, width = master.shape
    tile = min(128, rows)
    spec = pl.BlockSpec((tile, width), lambda i: (i, 0))
    blocks = width // BLK
    return pl.pallas_call(
        update_kernel,
        out_shape=(
            jax.ShapeDtypeStruct((rows, width), BF16),
            jax.ShapeDtypeStruct((rows, blocks), F32),
            jax.ShapeDtypeStruct((rows, width), F32),
            jax.ShapeDtypeStruct((rows, width), F32),
            jax.ShapeDtypeStruct((rows, width), F32),
        ),
        grid=(rows // tile,),
        in_specs=[spec] * 6,
        out_specs=(spec, pl.BlockSpec((tile, blocks), lambda i: (i, 0)), spec, spec, spec),
        compiler_params=pltpu.CompilerParams(vmem_limit_bytes=32 * 1024 * 1024),
        name="update",
        cost_estimate=pl.CostEstimate(
            flops=20 * rows * width, bytes_accessed=32 * rows * width, transcendentals=rows * width
        ),
    )(own, left, right, master, first, second)


def shift(value, by):
    size = lax.axis_size("query")
    return lax.ppermute(value, "query", [(i, (i + by) % size) for i in range(size)])


def per_device(
    queries,
    positives,
    neg_clusters,
    owner_map,
    label_codes,
    label_scales,
    label_master,
    first_moment,
    second_moment,
):
    n_col, quarter, width = label_codes.shape
    crows = 4 * quarter
    half = n_col // 2
    my_y = lax.axis_index("query")
    my_col = lax.axis_index("cluster")

    own = dequantize(
        label_codes.reshape(n_col * quarter, width),
        label_scales.reshape(n_col * quarter, width // BLK),
    ).reshape(n_col, quarter, width)
    low, high = own[:half], own[half:]
    left_low = shift(low, 1)
    right_high = shift(high, -1)
    left_high = shift(high, 1)
    right_low = shift(low, -1)
    far_low = shift(left_low, 1)
    far_high = shift(right_high, -1)

    share = queries.shape[1] // 2
    query_rows = [
        lax.all_gather(queries[:, h * share : (h + 1) * share], "cluster", axis=1, tiled=True)[0]
        for h in range(2)
    ]
    neg_clusters, left_low, right_high = lax.optimization_barrier(
        (neg_clusters, left_low, right_high)
    )
    group_ids = lax.all_gather(neg_clusters, "cluster", axis=0, tiled=True).reshape(-1)

    places = my_col * n_col + jnp.arange(n_col, dtype=I32)
    all_ids = jnp.arange(owner_map.shape[0], dtype=I32)
    held = jnp.sum(jnp.where(owner_map[None, :] == places[:, None], all_ids[None, :], 0), axis=1)
    listed = jnp.sum((group_ids[None, :] == held[:, None]).astype(I32), axis=1)
    count = jnp.sum(listed)
    local = jnp.arange(n_col, dtype=I32)
    before = local[None, :] < local[:, None]
    ahead = jnp.sum(jnp.where(before, listed[None, :], 0), axis=1)
    rank = jnp.where(listed > 0, ahead, count + local - ahead)
    place = rank[None, :] == local[:, None]
    order = jnp.sum(jnp.where(place, local[None, :], 0), axis=1)
    base = jnp.sum(jnp.where(place, held[None, :], 0), axis=1) * crows
    info = jnp.stack([count, my_y.astype(I32)])
    by_half = positives[0].reshape(-1, 2, share)
    quarters = (own, right_low, far_low, far_high, left_low, left_high, right_high)
    query_grads, label_part = [], None
    for h in range(2):
        pid = jnp.broadcast_to(by_half[:, h].reshape(-1, 1), (query_rows[h].shape[0], 128))
        query_part, label_part = score_and_grads(
            order, base, info, query_rows[h], pid, quarters, label_part
        )
        query_grads.append(
            lax.psum_scatter(query_part, "cluster", scatter_dimension=0, tiled=True)
        )
    query_grad = jnp.concatenate(query_grads).astype(F32)

    via_left = shift(label_part[2, :half], 1)
    via_right = shift(label_part[2, half:], -1)
    left_b = shift(label_part[1, half:], 1)
    right_b = shift(label_part[3, :half], -1)
    left_a = shift(label_part[1, :half] + via_left, 1)
    right_a = shift(label_part[3, half:] + via_right, -1)
    from_left = jnp.concatenate([left_a, left_b])
    from_right = jnp.concatenate([right_b, right_a])

    flat = lambda value: value.reshape(n_col * quarter, width)
    new_codes, new_scales, new_master, new_first, new_second = update(
        flat(label_part[0]),
        flat(from_left),
        flat(from_right),
        flat(label_master),
        flat(first_moment),
        flat(second_moment),
    )
    shape = label_master.shape
    return (
        query_grad[None],
        new_codes.reshape(shape),
        new_scales.reshape(n_col, quarter, width // BLK),
        new_master.reshape(shape),
        new_first.reshape(shape),
        new_second.reshape(shape),
    )


def solution(mesh):
    in_specs = (
        P("query", "cluster", None),
        P("query", None),
        P("query", "cluster"),
        P(),
        P("cluster", "query", None),
        P("cluster", "query", None),
        P("cluster", "query", None),
        P("cluster", "query", None),
        P("cluster", "query", None),
    )
    out_specs = (
        P("query", "cluster", None),
        P("cluster", "query", None),
        P("cluster", "query", None),
        P("cluster", "query", None),
        P("cluster", "query", None),
        P("cluster", "query", None),
    )
    return jax.shard_map(
        per_device, mesh=mesh, in_specs=in_specs, out_specs=out_specs, check_vma=False
    )
```

```python
import functools
import math

import jax
import jax.numpy as jnp
from jax import lax
from jax.experimental import pallas as pl
from jax.experimental.pallas import tpu as pltpu
from jax.sharding import PartitionSpec as P

BLK = 128

pos_weight = 64.0
beta_first = 0.9
beta_second = 0.95
learn_rate = 0.05
adam_eps = 1e-08
adam_step = 20.0
scale_eps = 1e-06

STEP = 4
SUB = 512
FLIP = 512
SPLIT1, SPLIT2, SPLIT3 = 1,1,1

F32, BF16, I32 = jnp.float32, jnp.bfloat16, jnp.int32
ANY = pl.BlockSpec(memory_space=pl.ANY)
VMEM_LIMIT = 62 * 1024 * 1024


def dequant_kernel(codes_ref, scales_ref, rows_ref):
    rows, width = codes_ref.shape
    for blk in range(width // BLK):
        cols = slice(blk * BLK, (blk + 1) * BLK)
        scale = jnp.broadcast_to(scales_ref[:, blk : blk + 1], (rows, BLK))
        rows_ref[:, cols] = (codes_ref[:, cols].astype(F32) * scale).astype(BF16)


def dequantize(codes, scales):
    rows, width = codes.shape
    tile = min(256, rows)
    return pl.pallas_call(
        dequant_kernel,
        out_shape=jax.ShapeDtypeStruct((rows, width), BF16),
        grid=(rows // tile,),
        in_specs=[
            pl.BlockSpec((tile, width), lambda i: (i, 0)),
            pl.BlockSpec((tile, scales.shape[1]), lambda i: (i, 0)),
        ],
        out_specs=pl.BlockSpec((tile, width), lambda i: (i, 0)),
        name="dequantize",
        cost_estimate=pl.CostEstimate(
            flops=rows * width, bytes_accessed=4 * rows * width, transcendentals=0
        ),
    )(codes, scales)


def score_kernel(
    order_ref, base_ref, info_ref, q_hbm, pid_hbm, own_hbm, right_hbm, left_hbm, low_hbm, high_hbm,
    mine_u, mine_v, part_u, part_v, lab_own, lab_a, lab_b, lab_c, lab_d,
    q_ref, qt_ref, ids_ref, pid_ref, w_ref, acc_ref, wb_ref, id_ref, sa_ref, sb_ref,
    pa_ref, pb_ref, lt_ref, lab_ref, qg_ref, sem, q_sem, lab_sem, out_sem,
):
    total, width = q_ref.shape
    n_col, quarter = w_ref.shape[0] // 4, w_ref.shape[1]
    half = n_col // 2
    crows = 4 * quarter
    rows = STEP * crows
    n_pair = total // (2 * SUB)
    inv_root = 1.0 / math.sqrt(width)
    power_scale = math.log2(math.e) * inv_root
    listed = info_ref[0]
    my_y = info_ref[1]
    n_block = lax.div(listed + STEP - 1, STEP)

    def rows_of(start, size):
        return pl.ds(pl.multiple_of(start, size), size)

    load_q = [
        pltpu.make_async_copy(
            q_hbm.at[pl.ds(i * FLIP, FLIP)], q_ref.at[pl.ds(i * FLIP, FLIP)], q_sem.at[i]
        )
        for i in range(total // FLIP)
    ]
    targets = ((0, n_col), (n_col, n_col), (3 * n_col, n_col), (2 * n_col, half), (2 * n_col + half, half))
    pieces = (own_hbm, right_hbm, left_hbm, low_hbm, high_hbm)
    loads = [
        pltpu.make_async_copy(src, w_ref.at[pl.ds(*at)], sem.at[i])
        for i, (src, at) in enumerate(zip(pieces, targets, strict=True))
    ]
    load_ids = pltpu.make_async_copy(pid_hbm, ids_ref, sem.at[5])
    load_ids.start()
    for copy in load_q + loads:
        copy.start()

    def clear(entry, carry):
        where = order_ref[entry]
        for j in range(4):
            lab_ref[j * n_col + where] = jnp.zeros((quarter, width), BF16)
        return carry

    lax.fori_loop(listed, n_col, clear, 0)

    load_ids.wait()

    def spread(i, carry):
        row = jnp.broadcast_to(ids_ref[pl.ds(i, 1), :], (128, 128))
        pid_ref[rows_of(i * 128, 128), :] = row.T
        return carry

    lax.fori_loop(0, total // 128, spread, 0)

    for i, copy in enumerate(load_q):
        copy.wait()

        def flip(k, carry, i=i):
            at = rows_of(i * FLIP + k * 256, 256)
            qt_ref[:, at] = q_ref[at, :].T
            return carry

        lax.fori_loop(0, FLIP // 256, flip, 0)

    for copy in loads:
        copy.wait()

    lane = lax.broadcasted_iota(I32, (8, rows), 1)
    slot = lax.div(lane, jnp.full_like(lane, crows))
    within = lax.rem(lane, jnp.full_like(lane, crows))
    part = lax.rem(lax.div(within, jnp.full_like(lane, quarter)) + my_y, jnp.full_like(lane, 4))
    row_id = part * quarter + lax.rem(within, jnp.full_like(lane, quarter))

    def stage(block):
        buf = lax.rem(block, 2)
        ids = row_id
        for k in range(STEP):
            entry = jnp.minimum(block * STEP + k, n_col - 1)
            valid = block * STEP + k < listed
            where = order_ref[entry]
            ids = ids + jnp.where(slot == k, base_ref[entry], 0)
            for j in range(4):
                start = k * crows + j * quarter
                held = w_ref[j * n_col + where]
                wb_ref[buf, start : start + quarter, :] = jnp.where(
                    valid, held, jnp.zeros_like(held)
                )
        id_ref[buf] = ids

    def score(block, start, to_ref):
        size = SUB // SPLIT1
        for h in range(SPLIT1):
            to_ref[h * size : (h + 1) * size] = lax.dot_general(
                q_ref[rows_of(start + h * size, size), :],
                wb_ref[lax.rem(block, 2)],
                (((1,), (1,)), ((), ())),
                preferred_element_type=F32,
            )

    def slopes(block, start, from_ref, to_ref):
        pid = pid_ref[rows_of(start, SUB), :]
        ids = id_ref[lax.rem(block, 2)]
        for c in range(rows // 128):
            cols = slice(c * 128, (c + 1) * 128)
            hit = pid == ids[0:1, cols]
            power = from_ref[:, cols] * jnp.where(hit, power_scale, -power_scale)
            prob = jnp.where(hit, -pos_weight, 1.0) / (1.0 + jnp.exp2(power))
            to_ref[:, cols] = prob.astype(BF16)

    def grads(block, start, p_ref, lt_is_new):
        size = SUB // SPLIT2
        for h in range(SPLIT2):
            at = rows_of(start + h * size, size)
            old = jnp.where(block == 0, 0.0, acc_ref[at, :])
            acc_ref[at, :] = old + jnp.dot(
                p_ref[h * size : (h + 1) * size],
                wb_ref[lax.rem(block, 2)],
                preferred_element_type=F32,
            )
        buf = lax.rem(block, 2)
        size = width // SPLIT3
        for h in range(SPLIT3):
            cols = slice(h * size, (h + 1) * size)
            old = jnp.where(lt_is_new, 0.0, lt_ref[buf, cols])
            lt_ref[buf, cols] = old + jnp.dot(
                qt_ref[cols, rows_of(start, SUB)], p_ref[...], preferred_element_type=F32
            )

    def emit(block):
        lab = (lt_ref[lax.rem(block, 2)] * inv_root).T
        for k in range(STEP):
            entry = block * STEP + k

            @pl.when(entry < listed)
            def _(k=k, entry=entry):
                where = order_ref[entry]
                for j in range(4):
                    start = k * crows + j * quarter
                    lab_ref[j * n_col + where] = lab[start : start + quarter, :].astype(BF16)

    @pl.when(n_block > 0)
    def _():
        stage(0)
        score(0, 0, sa_ref)
        pb_ref[...] = jnp.zeros_like(pb_ref)

    def pair(t, carry):
        block, at = lax.div(t, n_pair), lax.rem(t, n_pair)
        before = jnp.maximum(t - 1, 0)
        pblock, pat = lax.div(before, n_pair), lax.rem(before, n_pair)
        nblock, nat = lax.div(t + 1, n_pair), lax.rem(t + 1, n_pair)
        here = at * (2 * SUB)

        @pl.when(nat == 0)
        def _():
            stage(nblock)

        @pl.when((at == 1) & (block > 0))
        def _():
            emit(block - 1)

        slopes(block, here, sa_ref, pa_ref)
        score(block, here + SUB, sb_ref)
        grads(pblock, pat * (2 * SUB) + SUB, pb_ref, False)
        slopes(block, here + SUB, sb_ref, pb_ref)
        score(nblock, nat * (2 * SUB), sa_ref)
        grads(block, here, pa_ref, at == 0)
        return carry

    lax.fori_loop(0, n_block * n_pair, pair, 0)

    @pl.when(n_block > 0)
    def _():
        grads(n_block - 1, total - SUB, pb_ref, False)
        emit(n_block - 1)

    put_lab = []
    at = 0
    for i, out in enumerate((lab_own, lab_a, lab_b, lab_c, lab_d)):
        size = out.shape[0]
        put_lab.append(pltpu.make_async_copy(lab_ref.at[pl.ds(at, size)], out, lab_sem.at[i]))
        put_lab[-1].start()
        at += size

    my_col = info_ref[2]
    my_x, my_z, my_core = lax.div(my_col, 8), lax.rem(lax.div(my_col, 2), 4), lax.rem(my_col, 2)
    share = total // 32
    part_rows = share // 2

    def puts(k, out_u, out_v):
        x, z = lax.rem(lax.div(k, 8) + 4 - my_x, 4), lax.rem(lax.div(k, 2) + 8 - my_z, 4)
        return (
            pltpu.make_async_copy(
                qg_ref.at[rows_of(k * share, part_rows)], out_u.at[x * 4 + z], out_sem.at[0, k]
            ),
            pltpu.make_async_copy(
                qg_ref.at[rows_of(k * share + part_rows, part_rows)],
                out_v.at[z * 4 + x],
                out_sem.at[1, k],
            ),
        )

    def finish(k, carry):
        at = rows_of(k * share, share)
        qg_ref[at, :] = jnp.where(n_block > 0, acc_ref[at, :] * inv_root, 0.0).astype(BF16)

        @pl.when(lax.rem(k, 2) == my_core)
        def _():
            for copy in puts(k, mine_u, mine_v):
                copy.start()

        @pl.when(lax.rem(k, 2) != my_core)
        def _():
            for copy in puts(k, part_u, part_v):
                copy.start()

        return carry

    lax.fori_loop(0, 32, finish, 0)

    def settle(k, carry):
        for copy in puts(k, mine_u, mine_v):
            copy.wait()
        return carry

    lax.fori_loop(0, 32, settle, 0)
    for copy in put_lab:
        copy.wait()


def score_and_grads(order, base, info, queries, pid, quarters):
    total, width = queries.shape
    n_col, quarter = quarters[0].shape[0], quarters[0].shape[1]
    half = n_col // 2
    block = STEP * 4 * quarter
    smem = pl.BlockSpec(memory_space=pltpu.SMEM)
    share = jax.ShapeDtypeStruct((16, total // 64, width), BF16)
    label = lambda size: jax.ShapeDtypeStruct((size, quarter, width), BF16)
    return pl.pallas_call(
        score_kernel,
        out_shape=(share,) * 4
        + (label(n_col), label(half), label(n_col), label(n_col), label(half)),
        in_specs=[smem] * 3 + [ANY] * 7,
        out_specs=(ANY,) * 9,
        scratch_shapes=[
            pltpu.VMEM((total, width), BF16),
            pltpu.VMEM((width, total), BF16),
            pltpu.VMEM((total // 128, 128), I32),
            pltpu.VMEM((total, 128), I32),
            pltpu.VMEM((4 * n_col, quarter, width), BF16),
            pltpu.VMEM((total, width), F32),
            pltpu.VMEM((2, block, width), BF16),
            pltpu.VMEM((2, 8, block), I32),
            pltpu.VMEM((SUB, block), F32),
            pltpu.VMEM((SUB, block), F32),
            pltpu.VMEM((SUB, block), BF16),
            pltpu.VMEM((SUB, block), BF16),
            pltpu.VMEM((2, width, block), F32),
            pltpu.VMEM((4 * n_col, quarter, width), BF16),
            pltpu.VMEM((total, width), BF16),
            pltpu.SemaphoreType.DMA((6,)),
            pltpu.SemaphoreType.DMA((total // FLIP,)),
            pltpu.SemaphoreType.DMA((5,)),
            pltpu.SemaphoreType.DMA((2, 32)),
        ],
        compiler_params=pltpu.CompilerParams(vmem_limit_bytes=VMEM_LIMIT),
        name="score",
        cost_estimate=pl.CostEstimate(
            flops=3 * total * n_col * 2 * quarter * width * 2,
            bytes_accessed=4 * total * width + 16 * n_col * quarter * width,
            transcendentals=total * n_col * 4 * quarter,
        ),
    )(order, base, info, queries, pid, *quarters)


def update_kernel(
    own_ref, left_ref, right_ref, master_ref, first_ref, second_ref,
    codes_ref, scales_ref, master_out, first_out, second_out,
):
    width = master_ref.shape[1]
    fix_first = 1.0 - beta_first**adam_step
    fix_second = 1.0 - beta_second**adam_step
    peaks = []
    for blk in range(width // BLK):
        cols = slice(blk * BLK, (blk + 1) * BLK)
        grad = (
            own_ref[:, cols].astype(F32)
            + left_ref[:, cols].astype(F32)
            + right_ref[:, cols].astype(F32)
        )
        first = beta_first * first_ref[:, cols] + (1.0 - beta_first) * grad
        second = beta_second * second_ref[:, cols] + (1.0 - beta_second) * grad * grad
        master = master_ref[:, cols] - learn_rate * (first / fix_first) / (
            jnp.sqrt(second / fix_second) + adam_eps
        )
        peak = jnp.max(jnp.abs(master), axis=1, keepdims=True) + scale_eps
        codes_ref[:, cols] = (master / peak).astype(BF16)
        master_out[:, cols] = master
        first_out[:, cols] = first
        second_out[:, cols] = second
        peaks.append(peak)
    scales_ref[...] = jnp.concatenate(peaks, axis=1)


def update(own, left, right, master, first, second):
    rows, width = master.shape
    tile = min(128, rows)
    spec = pl.BlockSpec((tile, width), lambda i: (i, 0))
    blocks = width // BLK
    return pl.pallas_call(
        update_kernel,
        out_shape=(
            jax.ShapeDtypeStruct((rows, width), BF16),
            jax.ShapeDtypeStruct((rows, blocks), F32),
            jax.ShapeDtypeStruct((rows, width), F32),
            jax.ShapeDtypeStruct((rows, width), F32),
            jax.ShapeDtypeStruct((rows, width), F32),
        ),
        grid=(rows // tile,),
        in_specs=[spec] * 6,
        out_specs=(spec, pl.BlockSpec((tile, blocks), lambda i: (i, 0)), spec, spec, spec),
        compiler_params=pltpu.CompilerParams(vmem_limit_bytes=32 * 1024 * 1024),
        name="update",
        cost_estimate=pl.CostEstimate(
            flops=20 * rows * width, bytes_accessed=32 * rows * width, transcendentals=rows * width
        ),
    )(own, left, right, master, first, second)


def shift(value, by):
    size = lax.axis_size("query")
    return lax.ppermute(value, "query", [(i, (i + by) % size) for i in range(size)])


def place(x, z, core):
    return (x % 4 * 4 + z % 4) * 2 + core


def hop(value, x=0, z=0, core=0):
    pairs = [
        (place(a, b, c), place(a + x, b + z, c ^ core))
        for a in range(4)
        for b in range(4)
        for c in range(2)
    ]
    return lax.ppermute(value, "cluster", pairs)


def add(*values):
    return sum(value.astype(F32) for value in values).astype(BF16)


def ring_sum(own, a, b, c, d, send):
    half = a.shape[0]
    left, right = send(b, 1), send(c, -1)
    left_low = send(add(a, left[half:]), 1)
    right_high = send(add(d, right[:half]), -1)
    return (own, jnp.concatenate([left_low, left[:half]]), jnp.concatenate([right[half:], right_high]))


def cut(value):
    n = value.shape[0] // 4
    half = n // 2
    return value[:n], value[n : n + half], value[n + half : 2 * n + half], value[2 * n + half : 4 * n - half], value[4 * n - half :]


def ring_sum_small(value, send):
    n = value.shape[0] // 4
    parts = [send(value[j * n : (j + 1) * n], j if j < 3 else -1) for j in range(1, 4)]
    return add(value[:n], *parts)


def scatter_queries(mine_u, mine_v, part_u, part_v):
    along_x = lambda value, by: hop(value, x=by)
    along_z = lambda value, by: hop(value, z=by)
    u = add(mine_u, hop(part_u, core=1))
    v = add(mine_v, hop(part_v, core=1))
    u = add(*ring_sum(*cut(u), along_x))
    v = add(*ring_sum(*cut(v), along_z))
    u = ring_sum_small(u, along_z)
    v = ring_sum_small(v, along_x)
    return jnp.concatenate([u[0], v[0]])


def per_device(
    queries,
    positives,
    neg_clusters,
    owner_map,
    label_codes,
    label_scales,
    label_master,
    first_moment,
    second_moment,
):
    n_col, quarter, width = label_codes.shape
    crows = 4 * quarter
    half = n_col // 2
    my_y = lax.axis_index("query")
    my_col = lax.axis_index("cluster")

    own = dequantize(
        label_codes.reshape(n_col * quarter, width),
        label_scales.reshape(n_col * quarter, width // BLK),
    ).reshape(n_col, quarter, width)
    left, right = shift(own, 1), shift(own, -1)
    far_low, far_high = shift(left[:half], 1), shift(right[half:], -1)

    query_rows = lax.all_gather(queries, "cluster", axis=1, tiled=True)[0]
    group_ids = lax.all_gather(neg_clusters, "cluster", axis=0, tiled=True).reshape(-1)

    places = my_col * n_col + jnp.arange(n_col, dtype=I32)
    all_ids = jnp.arange(owner_map.shape[0], dtype=I32)
    held = jnp.sum(jnp.where(owner_map[None, :] == places[:, None], all_ids[None, :], 0), axis=1)
    listed = jnp.sum((group_ids[None, :] == held[:, None]).astype(I32), axis=1)
    count = jnp.sum(listed)
    local = jnp.arange(n_col, dtype=I32)
    before = local[None, :] < local[:, None]
    ahead = jnp.sum(jnp.where(before, listed[None, :], 0), axis=1)
    rank = jnp.where(listed > 0, ahead, count + local - ahead)
    place = rank[None, :] == local[:, None]
    order = jnp.sum(jnp.where(place, local[None, :], 0), axis=1)
    base = jnp.sum(jnp.where(place, held[None, :], 0), axis=1) * crows
    info = jnp.stack([count, my_y.astype(I32), my_col.astype(I32)])
    *query_parts, label_own, label_a, label_b, label_c, label_d = score_and_grads(
        order,
        base,
        info,
        query_rows,
        positives.reshape(-1, 128),
        (own, right, left, far_low, far_high),
    )
    label_parts = ring_sum(label_own, label_a, label_b, label_c, label_d, shift)
    query_grad = scatter_queries(*query_parts).astype(F32)

    flat = lambda value: value.reshape(n_col * quarter, width)
    new_codes, new_scales, new_master, new_first, new_second = update(
        *(flat(part) for part in label_parts),
        flat(label_master),
        flat(first_moment),
        flat(second_moment),
    )
    shape = label_master.shape
    return (
        query_grad[None],
        new_codes.reshape(shape),
        new_scales.reshape(n_col, quarter, width // BLK),
        new_master.reshape(shape),
        new_first.reshape(shape),
        new_second.reshape(shape),
    )


def solution(mesh):
    in_specs = (
        P("query", "cluster", None),
        P("query", None),
        P("query", "cluster"),
        P(),
        P("cluster", "query", None),
        P("cluster", "query", None),
        P("cluster", "query", None),
        P("cluster", "query", None),
        P("cluster", "query", None),
    )
    out_specs = (
        P("query", "cluster", None),
        P("cluster", "query", None),
        P("cluster", "query", None),
        P("cluster", "query", None),
        P("cluster", "query", None),
        P("cluster", "query", None),
    )
    return jax.shard_map(
        per_device, mesh=mesh, in_specs=in_specs, out_specs=out_specs, check_vma=False
    )
```

```python
import functools
import math

import jax
import jax.numpy as jnp
from jax import lax
from jax.experimental import pallas as pl
from jax.experimental.pallas import tpu as pltpu
from jax.sharding import PartitionSpec as P

BLK = 128

pos_weight = 64.0
beta_first = 0.9
beta_second = 0.95
learn_rate = 0.05
adam_eps = 1e-08
adam_step = 20.0
scale_eps = 1e-06

STEP = 4
SUB = 512
FLIP = 512
SPLIT1, SPLIT2, SPLIT3 = 1,1,1

F32, BF16, I32 = jnp.float32, jnp.bfloat16, jnp.int32
ANY = pl.BlockSpec(memory_space=pl.ANY)
VMEM_LIMIT = 62 * 1024 * 1024


def dequant_kernel(codes_ref, scales_ref, rows_ref):
    rows, width = codes_ref.shape
    for blk in range(width // BLK):
        cols = slice(blk * BLK, (blk + 1) * BLK)
        scale = jnp.broadcast_to(scales_ref[:, blk : blk + 1], (rows, BLK))
        rows_ref[:, cols] = (codes_ref[:, cols].astype(F32) * scale).astype(BF16)


def dequantize(codes, scales):
    rows, width = codes.shape
    tile = min(256, rows)
    return pl.pallas_call(
        dequant_kernel,
        out_shape=jax.ShapeDtypeStruct((rows, width), BF16),
        grid=(rows // tile,),
        in_specs=[
            pl.BlockSpec((tile, width), lambda i: (i, 0)),
            pl.BlockSpec((tile, scales.shape[1]), lambda i: (i, 0)),
        ],
        out_specs=pl.BlockSpec((tile, width), lambda i: (i, 0)),
        name="dequantize",
        cost_estimate=pl.CostEstimate(
            flops=rows * width, bytes_accessed=4 * rows * width, transcendentals=0
        ),
    )(codes, scales)


def score_kernel(
    order_ref, base_ref, info_ref, q_hbm, pid_hbm, own_hbm, right_hbm, left_hbm, low_hbm, high_hbm,
    mine_u, mine_v, part_u, part_v, lab_own, lab_a, lab_b, lab_c, lab_d,
    q_ref, qt_ref, ids_ref, pid_ref, w_ref, acc_ref, wb_ref, id_ref, sa_ref, sb_ref,
    pa_ref, pb_ref, lt_ref, lab_ref, qg_ref, sem, q_sem, lab_sem, out_sem,
):
    total, width = q_ref.shape
    n_col, quarter = w_ref.shape[0] // 4, w_ref.shape[1]
    half = n_col // 2
    crows = 4 * quarter
    rows = STEP * crows
    n_pair = total // (2 * SUB)
    inv_root = 1.0 / math.sqrt(width)
    power_scale = math.log2(math.e) * inv_root
    listed = info_ref[0]
    my_y = info_ref[1]
    n_block = lax.div(listed + STEP - 1, STEP)

    def rows_of(start, size):
        return pl.ds(pl.multiple_of(start, size), size)

    load_q = [
        pltpu.make_async_copy(
            q_hbm.at[pl.ds(i * FLIP, FLIP)], q_ref.at[pl.ds(i * FLIP, FLIP)], q_sem.at[i]
        )
        for i in range(total // FLIP)
    ]
    targets = ((0, n_col), (n_col, n_col), (3 * n_col, n_col), (2 * n_col, half), (2 * n_col + half, half))
    pieces = (own_hbm, right_hbm, left_hbm, low_hbm, high_hbm)
    loads = [
        pltpu.make_async_copy(src, w_ref.at[pl.ds(*at)], sem.at[i])
        for i, (src, at) in enumerate(zip(pieces, targets, strict=True))
    ]
    load_ids = pltpu.make_async_copy(pid_hbm, ids_ref, sem.at[5])
    load_ids.start()
    for copy in load_q + loads:
        copy.start()

    def clear(entry, carry):
        where = order_ref[entry]
        for j in range(4):
            lab_ref[j * n_col + where] = jnp.zeros((quarter, width), BF16)
        return carry

    lax.fori_loop(listed, n_col, clear, 0)

    load_ids.wait()

    def spread(i, carry):
        row = jnp.broadcast_to(ids_ref[pl.ds(i, 1), :], (128, 128))
        pid_ref[rows_of(i * 128, 128), :] = row.T
        return carry

    lax.fori_loop(0, total // 128, spread, 0)

    for i, copy in enumerate(load_q):
        copy.wait()

        def flip(k, carry, i=i):
            at = rows_of(i * FLIP + k * 256, 256)
            qt_ref[:, at] = q_ref[at, :].T
            return carry

        lax.fori_loop(0, FLIP // 256, flip, 0)

    for copy in loads:
        copy.wait()

    lane = lax.broadcasted_iota(I32, (8, rows), 1)
    slot = lax.div(lane, jnp.full_like(lane, crows))
    within = lax.rem(lane, jnp.full_like(lane, crows))
    part = lax.rem(lax.div(within, jnp.full_like(lane, quarter)) + my_y, jnp.full_like(lane, 4))
    row_id = part * quarter + lax.rem(within, jnp.full_like(lane, quarter))

    def stage(block):
        buf = lax.rem(block, 2)
        ids = row_id
        for k in range(STEP):
            entry = jnp.minimum(block * STEP + k, n_col - 1)
            valid = block * STEP + k < listed
            where = order_ref[entry]
            ids = ids + jnp.where(slot == k, base_ref[entry], 0)
            for j in range(4):
                start = k * crows + j * quarter
                held = w_ref[j * n_col + where]
                wb_ref[buf, start : start + quarter, :] = jnp.where(
                    valid, held, jnp.zeros_like(held)
                )
        id_ref[buf] = ids

    def score(block, start, to_ref):
        size = SUB // SPLIT1
        for h in range(SPLIT1):
            to_ref[h * size : (h + 1) * size] = lax.dot_general(
                q_ref[rows_of(start + h * size, size), :],
                wb_ref[lax.rem(block, 2)],
                (((1,), (1,)), ((), ())),
                preferred_element_type=F32,
            )

    def slopes(block, start, from_ref, to_ref):
        pid = pid_ref[rows_of(start, SUB), :]
        ids = id_ref[lax.rem(block, 2)]
        for c in range(rows // 128):
            cols = slice(c * 128, (c + 1) * 128)
            hit = pid == ids[0:1, cols]
            power = from_ref[:, cols] * jnp.where(hit, power_scale, -power_scale)
            prob = jnp.where(hit, -pos_weight, 1.0) / (1.0 + jnp.exp2(power))
            to_ref[:, cols] = prob.astype(BF16)

    def grads(block, start, p_ref, lt_is_new):
        size = SUB // SPLIT2
        for h in range(SPLIT2):
            at = rows_of(start + h * size, size)
            old = jnp.where(block == 0, 0.0, acc_ref[at, :])
            acc_ref[at, :] = old + jnp.dot(
                p_ref[h * size : (h + 1) * size],
                wb_ref[lax.rem(block, 2)],
                preferred_element_type=F32,
            )
        buf = lax.rem(block, 2)
        size = width // SPLIT3
        for h in range(SPLIT3):
            cols = slice(h * size, (h + 1) * size)
            old = jnp.where(lt_is_new, 0.0, lt_ref[buf, cols])
            lt_ref[buf, cols] = old + jnp.dot(
                qt_ref[cols, rows_of(start, SUB)], p_ref[...], preferred_element_type=F32
            )

    def emit(block):
        lab = (lt_ref[lax.rem(block, 2)] * inv_root).T
        for k in range(STEP):
            entry = block * STEP + k

            @pl.when(entry < listed)
            def _(k=k, entry=entry):
                where = order_ref[entry]
                for j in range(4):
                    start = k * crows + j * quarter
                    lab_ref[j * n_col + where] = lab[start : start + quarter, :].astype(BF16)

    @pl.when(n_block > 0)
    def _():
        stage(0)
        score(0, 0, sa_ref)
        pb_ref[...] = jnp.zeros_like(pb_ref)

    def pair(t, carry):
        block, at = lax.div(t, n_pair), lax.rem(t, n_pair)
        before = jnp.maximum(t - 1, 0)
        pblock, pat = lax.div(before, n_pair), lax.rem(before, n_pair)
        nblock, nat = lax.div(t + 1, n_pair), lax.rem(t + 1, n_pair)
        here = at * (2 * SUB)

        @pl.when(nat == 0)
        def _():
            stage(nblock)

        @pl.when((at == 1) & (block > 0))
        def _():
            emit(block - 1)

        slopes(block, here, sa_ref, pa_ref)
        score(block, here + SUB, sb_ref)
        grads(pblock, pat * (2 * SUB) + SUB, pb_ref, False)
        slopes(block, here + SUB, sb_ref, pb_ref)
        score(nblock, nat * (2 * SUB), sa_ref)
        grads(block, here, pa_ref, at == 0)
        return carry

    lax.fori_loop(0, n_block * n_pair, pair, 0)

    @pl.when(n_block > 0)
    def _():
        grads(n_block - 1, total - SUB, pb_ref, False)
        emit(n_block - 1)

    put_lab = []
    at = 0
    for i, out in enumerate((lab_own, lab_a, lab_b, lab_c, lab_d)):
        size = out.shape[0]
        put_lab.append(pltpu.make_async_copy(lab_ref.at[pl.ds(at, size)], out, lab_sem.at[i]))
        put_lab[-1].start()
        at += size

    my_col = info_ref[2]
    my_x, my_z, my_core = lax.div(my_col, 8), lax.rem(lax.div(my_col, 2), 4), lax.rem(my_col, 2)
    share = total // 32
    part_rows = share // 2

    def puts(k, out_u, out_v):
        x, z = lax.rem(lax.div(k, 8) + 4 - my_x, 4), lax.rem(lax.div(k, 2) + 8 - my_z, 4)
        return (
            pltpu.make_async_copy(
                qg_ref.at[rows_of(k * share, part_rows)], out_u.at[x * 4 + z], out_sem.at[0, k]
            ),
            pltpu.make_async_copy(
                qg_ref.at[rows_of(k * share + part_rows, part_rows)],
                out_v.at[z * 4 + x],
                out_sem.at[1, k],
            ),
        )

    def finish(k, carry):
        at = rows_of(k * share, share)
        qg_ref[at, :] = jnp.where(n_block > 0, acc_ref[at, :] * inv_root, 0.0).astype(BF16)

        @pl.when(lax.rem(k, 2) == my_core)
        def _():
            for copy in puts(k, mine_u, mine_v):
                copy.start()

        @pl.when(lax.rem(k, 2) != my_core)
        def _():
            for copy in puts(k, part_u, part_v):
                copy.start()

        return carry

    lax.fori_loop(0, 32, finish, 0)

    def settle(k, carry):
        for copy in puts(k, mine_u, mine_v):
            copy.wait()
        return carry

    lax.fori_loop(0, 32, settle, 0)
    for copy in put_lab:
        copy.wait()


def score_and_grads(order, base, info, queries, pid, quarters):
    total, width = queries.shape
    n_col, quarter = quarters[0].shape[0], quarters[0].shape[1]
    half = n_col // 2
    block = STEP * 4 * quarter
    smem = pl.BlockSpec(memory_space=pltpu.SMEM)
    share = jax.ShapeDtypeStruct((16, total // 64, width), BF16)
    label = lambda size: jax.ShapeDtypeStruct((size, quarter, width), BF16)
    return pl.pallas_call(
        score_kernel,
        out_shape=(share,) * 4
        + (label(n_col), label(half), label(n_col), label(n_col), label(half)),
        in_specs=[smem] * 3 + [ANY] * 7,
        out_specs=(ANY,) * 9,
        scratch_shapes=[
            pltpu.VMEM((total, width), BF16),
            pltpu.VMEM((width, total), BF16),
            pltpu.VMEM((total // 128, 128), I32),
            pltpu.VMEM((total, 128), I32),
            pltpu.VMEM((4 * n_col, quarter, width), BF16),
            pltpu.VMEM((total, width), F32),
            pltpu.VMEM((2, block, width), BF16),
            pltpu.VMEM((2, 8, block), I32),
            pltpu.VMEM((SUB, block), F32),
            pltpu.VMEM((SUB, block), F32),
            pltpu.VMEM((SUB, block), BF16),
            pltpu.VMEM((SUB, block), BF16),
            pltpu.VMEM((2, width, block), F32),
            pltpu.VMEM((4 * n_col, quarter, width), BF16),
            pltpu.VMEM((total, width), BF16),
            pltpu.SemaphoreType.DMA((6,)),
            pltpu.SemaphoreType.DMA((total // FLIP,)),
            pltpu.SemaphoreType.DMA((5,)),
            pltpu.SemaphoreType.DMA((2, 32)),
        ],
        compiler_params=pltpu.CompilerParams(vmem_limit_bytes=VMEM_LIMIT),
        name="score",
        cost_estimate=pl.CostEstimate(
            flops=3 * total * n_col * 2 * quarter * width * 2,
            bytes_accessed=4 * total * width + 16 * n_col * quarter * width,
            transcendentals=total * n_col * 4 * quarter,
        ),
    )(order, base, info, queries, pid, *quarters)


def update_kernel(
    own_ref, left_ref, right_ref, master_ref, first_ref, second_ref,
    codes_ref, scales_ref, master_out, first_out, second_out,
):
    width = master_ref.shape[1]
    fix_first = 1.0 - beta_first**adam_step
    fix_second = 1.0 - beta_second**adam_step
    peaks = []
    for blk in range(width // BLK):
        cols = slice(blk * BLK, (blk + 1) * BLK)
        grad = (
            own_ref[:, cols].astype(F32)
            + left_ref[:, cols].astype(F32)
            + right_ref[:, cols].astype(F32)
        )
        first = beta_first * first_ref[:, cols] + (1.0 - beta_first) * grad
        second = beta_second * second_ref[:, cols] + (1.0 - beta_second) * grad * grad
        master = master_ref[:, cols] - learn_rate * (first / fix_first) / (
            jnp.sqrt(second / fix_second) + adam_eps
        )
        peak = jnp.max(jnp.abs(master), axis=1, keepdims=True) + scale_eps
        codes_ref[:, cols] = (master / peak).astype(BF16)
        master_out[:, cols] = master
        first_out[:, cols] = first
        second_out[:, cols] = second
        peaks.append(peak)
    scales_ref[...] = jnp.concatenate(peaks, axis=1)


def update(own, left, right, master, first, second):
    rows, width = master.shape
    tile = min(128, rows)
    spec = pl.BlockSpec((tile, width), lambda i: (i, 0))
    blocks = width // BLK
    return pl.pallas_call(
        update_kernel,
        out_shape=(
            jax.ShapeDtypeStruct((rows, width), BF16),
            jax.ShapeDtypeStruct((rows, blocks), F32),
            jax.ShapeDtypeStruct((rows, width), F32),
            jax.ShapeDtypeStruct((rows, width), F32),
            jax.ShapeDtypeStruct((rows, width), F32),
        ),
        grid=(rows // tile,),
        in_specs=[spec] * 6,
        out_specs=(spec, pl.BlockSpec((tile, blocks), lambda i: (i, 0)), spec, spec, spec),
        compiler_params=pltpu.CompilerParams(vmem_limit_bytes=32 * 1024 * 1024),
        name="update",
        cost_estimate=pl.CostEstimate(
            flops=20 * rows * width, bytes_accessed=32 * rows * width, transcendentals=rows * width
        ),
    )(own, left, right, master, first, second)


def shift(value, by):
    size = lax.axis_size("query")
    return lax.ppermute(value, "query", [(i, (i + by) % size) for i in range(size)])


def place(x, z, core):
    return (x % 4 * 4 + z % 4) * 2 + core


def hop(value, x=0, z=0, core=0):
    pairs = [
        (place(a, b, c), place(a + x, b + z, c ^ core))
        for a in range(4)
        for b in range(4)
        for c in range(2)
    ]
    return lax.ppermute(value, "cluster", pairs)


def add(*values):
    return sum(value.astype(F32) for value in values).astype(BF16)


def ring_open(b, c, send):
    return send(b, 1), send(c, -1)


def ring_close(own, a, d, left, right, send):
    half = a.shape[0]
    left_low = send(add(a, left[half:]), 1)
    right_high = send(add(d, right[:half]), -1)
    return (own, jnp.concatenate([left_low, left[:half]]), jnp.concatenate([right[half:], right_high]))


def ring_sum(value, send):
    own, a, b, c, d = cut(value)
    return add(*ring_close(own, a, d, *ring_open(b, c, send), send))


def cut(value):
    n = value.shape[0] // 4
    half = n // 2
    return value[:n], value[n : n + half], value[n + half : 2 * n + half], value[2 * n + half : 4 * n - half], value[4 * n - half :]


def ring_sum_small(value, send):
    n = value.shape[0] // 4
    parts = [send(value[j * n : (j + 1) * n], j if j < 3 else -1) for j in range(1, 4)]
    return add(value[:n], *parts)


def along_x(value, by):
    return hop(value, x=by)


def along_z(value, by):
    return hop(value, z=by)


def per_device(
    queries,
    positives,
    neg_clusters,
    owner_map,
    label_codes,
    label_scales,
    label_master,
    first_moment,
    second_moment,
):
    n_col, quarter, width = label_codes.shape
    crows = 4 * quarter
    half = n_col // 2
    my_y = lax.axis_index("query")
    my_col = lax.axis_index("cluster")

    own = dequantize(
        label_codes.reshape(n_col * quarter, width),
        label_scales.reshape(n_col * quarter, width // BLK),
    ).reshape(n_col, quarter, width)
    left, right = shift(own, 1), shift(own, -1)
    far_low, far_high = shift(left[:half], 1), shift(right[half:], -1)

    query_rows = lax.all_gather(queries, "cluster", axis=1, tiled=True)[0]
    group_ids = lax.all_gather(neg_clusters, "cluster", axis=0, tiled=True).reshape(-1)

    places = my_col * n_col + jnp.arange(n_col, dtype=I32)
    all_ids = jnp.arange(owner_map.shape[0], dtype=I32)
    held = jnp.sum(jnp.where(owner_map[None, :] == places[:, None], all_ids[None, :], 0), axis=1)
    listed = jnp.sum((group_ids[None, :] == held[:, None]).astype(I32), axis=1)
    count = jnp.sum(listed)
    local = jnp.arange(n_col, dtype=I32)
    before = local[None, :] < local[:, None]
    ahead = jnp.sum(jnp.where(before, listed[None, :], 0), axis=1)
    rank = jnp.where(listed > 0, ahead, count + local - ahead)
    place = rank[None, :] == local[:, None]
    order = jnp.sum(jnp.where(place, local[None, :], 0), axis=1)
    base = jnp.sum(jnp.where(place, held[None, :], 0), axis=1) * crows
    info = jnp.stack([count, my_y.astype(I32), my_col.astype(I32)])
    *query_parts, label_own, label_a, label_b, label_c, label_d = score_and_grads(
        order,
        base,
        info,
        query_rows,
        positives.reshape(-1, 128),
        (own, right, left, far_low, far_high),
    )
    label_hops = ring_open(label_b, label_c, shift)
    mine_u, mine_v, part_u, part_v = query_parts
    u = add(mine_u, hop(part_u, core=1))
    v = add(mine_v, hop(part_v, core=1))
    u = ring_sum(u, along_x)
    v = ring_sum(v, along_z)
    label_left, label_right, u, v = lax.optimization_barrier((*label_hops, u, v))
    label_parts = ring_close(label_own, label_a, label_d, label_left, label_right, shift)
    u = ring_sum_small(u, along_z)
    v = ring_sum_small(v, along_x)
    query_grad = jnp.concatenate([u[0], v[0]]).astype(F32)

    flat = lambda value: value.reshape(n_col * quarter, width)
    new_codes, new_scales, new_master, new_first, new_second = update(
        *(flat(part) for part in label_parts),
        flat(label_master),
        flat(first_moment),
        flat(second_moment),
    )
    shape = label_master.shape
    return (
        query_grad[None],
        new_codes.reshape(shape),
        new_scales.reshape(n_col, quarter, width // BLK),
        new_master.reshape(shape),
        new_first.reshape(shape),
        new_second.reshape(shape),
    )


def solution(mesh):
    in_specs = (
        P("query", "cluster", None),
        P("query", None),
        P("query", "cluster"),
        P(),
        P("cluster", "query", None),
        P("cluster", "query", None),
        P("cluster", "query", None),
        P("cluster", "query", None),
        P("cluster", "query", None),
    )
    out_specs = (
        P("query", "cluster", None),
        P("cluster", "query", None),
        P("cluster", "query", None),
        P("cluster", "query", None),
        P("cluster", "query", None),
        P("cluster", "query", None),
    )
    return jax.shard_map(
        per_device, mesh=mesh, in_specs=in_specs, out_specs=out_specs, check_vma=False
    )
```

```python
import math

import jax
import jax.numpy as jnp
from jax import lax
from jax.experimental import pallas as pl
from jax.experimental.pallas import tpu as pltpu
from jax.sharding import PartitionSpec as P


BLK = 128

pos_weight = 64.0
beta_first = 0.9
beta_second = 0.95
learn_rate = 0.05
adam_eps = 1e-08
adam_step = 20.0
scale_eps = 1e-06

STEP = 4
SUB = 512
ID_ROWS = 16
SPLIT1, SPLIT2, SPLIT3 = 1,1,1

F32, BF16, I32 = jnp.float32, jnp.bfloat16, jnp.int32
ANY = pl.BlockSpec(memory_space=pl.ANY)
VMEM_LIMIT = 62 * 1024 * 1024


def dequant_kernel(codes_ref, scales_ref, rows_ref):
    rows, width = codes_ref.shape
    for blk in range(width // BLK):
        cols = slice(blk * BLK, (blk + 1) * BLK)
        scale = jnp.broadcast_to(scales_ref[:, blk : blk + 1], (rows, BLK))
        rows_ref[:, cols] = (codes_ref[:, cols].astype(F32) * scale).astype(BF16)


def dequantize(codes, scales):
    rows, width = codes.shape
    tile = min(256, rows)
    return pl.pallas_call(
        dequant_kernel,
        out_shape=jax.ShapeDtypeStruct((rows, width), BF16),
        grid=(rows // tile,),
        in_specs=[
            pl.BlockSpec((tile, width), lambda i: (i, 0)),
            pl.BlockSpec((tile, scales.shape[1]), lambda i: (i, 0)),
        ],
        out_specs=pl.BlockSpec((tile, width), lambda i: (i, 0)),
        name="dequantize",
        cost_estimate=pl.CostEstimate(
            flops=rows * width, bytes_accessed=4 * rows * width, transcendentals=0
        ),
    )(codes, scales)


def score_kernel(
    order_ref, base_ref, info_ref, pid_hbm, own_hbm, right_hbm, left_hbm, low_hbm, high_hbm, *refs
):
    q_pieces, refs = (refs[:5], refs[5:10]), refs[10:]
    mine_u, mine_v, part_u, part_v, lab_own, lab_a, lab_b, lab_c, lab_d = refs[:9]
    q_ref, qt_ref, ids_ref, pid_ref, w_ref, acc_ref, wb_ref, id_ref, sa_ref, sb_ref = refs[9:19]
    pa_ref, pb_ref, lt_ref, lab_ref, qg_ref, sem, q_sem, lab_sem, out_sem = refs[19:]
    total, width = q_ref.shape
    n_col, quarter = w_ref.shape[0] // 4, w_ref.shape[1]
    half = n_col // 2
    crows = 4 * quarter
    rows = STEP * crows
    n_pair = total // (2 * SUB)
    inv_root = 1.0 / math.sqrt(width)
    power_scale = math.log2(math.e) * inv_root
    listed = info_ref[0]
    my_y = info_ref[1]
    n_block = lax.div(listed + STEP - 1, STEP)

    def rows_of(start, size):
        return pl.ds(pl.multiple_of(start, size), size)

    my_col = info_ref[2]
    my_x, my_z, my_core = lax.div(my_col, 8), lax.rem(lax.div(my_col, 2), 4), lax.rem(my_col, 2)
    share = total // 32

    load_q = []
    for core in range(2):
        own_q, right_q, left_q, low_q, high_q = q_pieces[core]
        for z, x in ((z, x) for z in range(4) for x in range(4)):
            src = (own_q, right_q, (low_q, high_q)[x // 2], left_q)[z].at[x % 2 if z == 2 else x]
            col = (lax.rem(my_x + x, 4) * 4 + lax.rem(my_z + z, 4)) * 2
            col = col + (my_core if core == 0 else 1 - my_core)
            load_q.append(
                pltpu.make_async_copy(
                    src.at[pl.ds(0, share)], q_ref.at[rows_of(col * share, share)], q_sem.at[col]
                )
            )
    targets = ((0, n_col), (n_col, n_col), (3 * n_col, n_col), (2 * n_col, half), (2 * n_col + half, half))
    pieces = (own_hbm, right_hbm, left_hbm, low_hbm, high_hbm)
    loads = [
        pltpu.make_async_copy(src, w_ref.at[pl.ds(*at)], sem.at[i])
        for i, (src, at) in enumerate(zip(pieces, targets, strict=True))
    ]
    load_ids = pltpu.make_async_copy(pid_hbm, ids_ref, sem.at[5])
    load_ids.start()
    for copy in load_q + loads:
        copy.start()

    def clear(entry, carry):
        where = order_ref[entry]
        for j in range(4):
            lab_ref[j * n_col + where] = jnp.zeros((quarter, width), BF16)
        return carry

    lax.fori_loop(listed, n_col, clear, 0)

    load_ids.wait()

    def spread(i, carry):
        row = jnp.broadcast_to(ids_ref[pl.ds(i, 1), :], (128, 128))
        pid_ref[rows_of(i * 128, 128), :] = row.T
        return carry

    lax.fori_loop(0, total // 128, spread, 0)

    def flip(i, carry):
        for h in range(2):
            k = 2 * i + h
            pltpu.make_async_copy(
                q_pieces[0][0].at[0, pl.ds(0, share)], q_ref.at[rows_of(k * share, share)], q_sem.at[k]
            ).wait()
        at = rows_of(i * 2 * share, 2 * share)
        qt_ref[:, at] = q_ref[at, :].T
        return carry

    lax.fori_loop(0, 16, flip, 0)

    for copy in loads:
        copy.wait()

    lane = lax.broadcasted_iota(I32, (8, rows), 1)
    slot = lax.div(lane, jnp.full_like(lane, crows))
    within = lax.rem(lane, jnp.full_like(lane, crows))
    part = lax.rem(lax.div(within, jnp.full_like(lane, quarter)) + my_y, jnp.full_like(lane, 4))
    row_id = part * quarter + lax.rem(within, jnp.full_like(lane, quarter))

    def stage(block):
        buf = lax.rem(block, 2)
        ids = row_id
        for k in range(STEP):
            entry = jnp.minimum(block * STEP + k, n_col - 1)
            valid = block * STEP + k < listed
            where = order_ref[entry]
            ids = ids + jnp.where(slot == k, base_ref[entry], 0)
            for j in range(4):
                start = k * crows + j * quarter
                held = w_ref[j * n_col + where]
                wb_ref[buf, start : start + quarter, :] = jnp.where(
                    valid, held, jnp.zeros_like(held)
                )
        id_ref[buf] = ids

    def score(block, start, to_ref):
        size = SUB // SPLIT1
        for h in range(SPLIT1):
            to_ref[h * size : (h + 1) * size] = lax.dot_general(
                q_ref[rows_of(start + h * size, size), :],
                wb_ref[lax.rem(block, 2)],
                (((1,), (1,)), ((), ())),
                preferred_element_type=F32,
            )

    def slopes(block, start, from_ref, to_ref):
        pid = pid_ref[rows_of(start, SUB), :]
        ids = id_ref[lax.rem(block, 2)]
        for c in range(rows // 128):
            cols = slice(c * 128, (c + 1) * 128)
            hit = pid == ids[0:1, cols]
            power = from_ref[:, cols] * jnp.where(hit, power_scale, -power_scale)
            prob = jnp.where(hit, -pos_weight, 1.0) / (1.0 + jnp.exp2(power))
            to_ref[:, cols] = prob.astype(BF16)

    def grads(block, start, p_ref, lt_is_new):
        size = SUB // SPLIT2
        for h in range(SPLIT2):
            at = rows_of(start + h * size, size)
            old = jnp.where(block == 0, 0.0, acc_ref[at, :])
            acc_ref[at, :] = old + jnp.dot(
                p_ref[h * size : (h + 1) * size],
                wb_ref[lax.rem(block, 2)],
                preferred_element_type=F32,
            )
        buf = lax.rem(block, 2)
        size = width // SPLIT3
        for h in range(SPLIT3):
            cols = slice(h * size, (h + 1) * size)
            old = jnp.where(lt_is_new, 0.0, lt_ref[buf, cols])
            lt_ref[buf, cols] = old + jnp.dot(
                qt_ref[cols, rows_of(start, SUB)], p_ref[...], preferred_element_type=F32
            )

    def emit(block):
        lab = (lt_ref[lax.rem(block, 2)] * inv_root).T
        for k in range(STEP):
            entry = block * STEP + k

            @pl.when(entry < listed)
            def _(k=k, entry=entry):
                where = order_ref[entry]
                for j in range(4):
                    start = k * crows + j * quarter
                    lab_ref[j * n_col + where] = lab[start : start + quarter, :].astype(BF16)

    @pl.when(n_block > 0)
    def _():
        stage(0)
        score(0, 0, sa_ref)
        pb_ref[...] = jnp.zeros_like(pb_ref)

    def pair(t, carry):
        block, at = lax.div(t, n_pair), lax.rem(t, n_pair)
        before = jnp.maximum(t - 1, 0)
        pblock, pat = lax.div(before, n_pair), lax.rem(before, n_pair)
        nblock, nat = lax.div(t + 1, n_pair), lax.rem(t + 1, n_pair)
        here = at * (2 * SUB)

        @pl.when(nat == 0)
        def _():
            stage(nblock)

        @pl.when((at == 1) & (block > 0))
        def _():
            emit(block - 1)

        slopes(block, here, sa_ref, pa_ref)
        score(block, here + SUB, sb_ref)
        grads(pblock, pat * (2 * SUB) + SUB, pb_ref, False)
        slopes(block, here + SUB, sb_ref, pb_ref)
        score(nblock, nat * (2 * SUB), sa_ref)
        grads(block, here, pa_ref, at == 0)
        return carry

    lax.fori_loop(0, n_block * n_pair, pair, 0)

    @pl.when(n_block > 0)
    def _():
        grads(n_block - 1, total - SUB, pb_ref, False)
        emit(n_block - 1)

    put_lab = []
    at = 0
    for i, out in enumerate((lab_own, lab_a, lab_b, lab_c, lab_d)):
        size = out.shape[0]
        put_lab.append(pltpu.make_async_copy(lab_ref.at[pl.ds(at, size)], out, lab_sem.at[i]))
        put_lab[-1].start()
        at += size

    part_rows = share // 2

    def puts(k, out_u, out_v):
        x, z = lax.rem(lax.div(k, 8) + 4 - my_x, 4), lax.rem(lax.div(k, 2) + 8 - my_z, 4)
        return (
            pltpu.make_async_copy(
                qg_ref.at[rows_of(k * share, part_rows)], out_u.at[x * 4 + z], out_sem.at[0, k]
            ),
            pltpu.make_async_copy(
                qg_ref.at[rows_of(k * share + part_rows, part_rows)],
                out_v.at[z * 4 + x],
                out_sem.at[1, k],
            ),
        )

    def finish(k, carry):
        at = rows_of(k * share, share)
        qg_ref[at, :] = jnp.where(n_block > 0, acc_ref[at, :] * inv_root, 0.0).astype(BF16)

        @pl.when(lax.rem(k, 2) == my_core)
        def _():
            for copy in puts(k, mine_u, mine_v):
                copy.start()

        @pl.when(lax.rem(k, 2) != my_core)
        def _():
            for copy in puts(k, part_u, part_v):
                copy.start()

        return carry

    lax.fori_loop(0, 32, finish, 0)

    def settle(k, carry):
        for copy in puts(k, mine_u, mine_v):
            copy.wait()
        return carry

    lax.fori_loop(0, 32, settle, 0)
    for copy in put_lab:
        copy.wait()


def score_and_grads(order, base, info, pid, quarters, queries):
    total, width = pid.size, quarters[0].shape[2]
    n_col, quarter = quarters[0].shape[0], quarters[0].shape[1]
    half = n_col // 2
    block = STEP * 4 * quarter
    smem = pl.BlockSpec(memory_space=pltpu.SMEM)
    share = jax.ShapeDtypeStruct((16, total // 64, width), BF16)
    label = lambda size: jax.ShapeDtypeStruct((size, quarter, width), BF16)
    return pl.pallas_call(
        score_kernel,
        out_shape=(share,) * 4
        + (label(n_col), label(half), label(n_col), label(n_col), label(half)),
        in_specs=[smem] * 3 + [ANY] * 16,
        out_specs=(ANY,) * 9,
        scratch_shapes=[
            pltpu.VMEM((total, width), BF16),
            pltpu.VMEM((width, total), BF16),
            pltpu.VMEM((total // 128, 128), I32),
            pltpu.VMEM((total, 128), I32),
            pltpu.VMEM((4 * n_col, quarter, width), BF16),
            pltpu.VMEM((total, width), F32),
            pltpu.VMEM((2, block, width), BF16),
            pltpu.VMEM((2, 8, block), I32),
            pltpu.VMEM((SUB, block), F32),
            pltpu.VMEM((SUB, block), F32),
            pltpu.VMEM((SUB, block), BF16),
            pltpu.VMEM((SUB, block), BF16),
            pltpu.VMEM((2, width, block), F32),
            pltpu.VMEM((4 * n_col, quarter, width), BF16),
            pltpu.VMEM((total, width), BF16),
            pltpu.SemaphoreType.DMA((6,)),
            pltpu.SemaphoreType.DMA((32,)),
            pltpu.SemaphoreType.DMA((5,)),
            pltpu.SemaphoreType.DMA((2, 32)),
        ],
        compiler_params=pltpu.CompilerParams(vmem_limit_bytes=VMEM_LIMIT),
        name="score",
        cost_estimate=pl.CostEstimate(
            flops=3 * total * n_col * 2 * quarter * width * 2,
            bytes_accessed=4 * total * width + 16 * n_col * quarter * width,
            transcendentals=total * n_col * 4 * quarter,
        ),
    )(order, base, info, pid, *quarters, *queries)


def update_kernel(
    own_ref, left_ref, right_ref, master_ref, first_ref, second_ref,
    codes_ref, scales_ref, master_out, first_out, second_out,
):
    width = master_ref.shape[1]
    fix_first = 1.0 - beta_first**adam_step
    fix_second = 1.0 - beta_second**adam_step
    peaks = []
    for blk in range(width // BLK):
        cols = slice(blk * BLK, (blk + 1) * BLK)
        grad = (
            own_ref[:, cols].astype(F32)
            + left_ref[:, cols].astype(F32)
            + right_ref[:, cols].astype(F32)
        )
        first = beta_first * first_ref[:, cols] + (1.0 - beta_first) * grad
        second = beta_second * second_ref[:, cols] + (1.0 - beta_second) * grad * grad
        master = master_ref[:, cols] - learn_rate * (first / fix_first) / (
            jnp.sqrt(second / fix_second) + adam_eps
        )
        peak = jnp.max(jnp.abs(master), axis=1, keepdims=True) + scale_eps
        codes_ref[:, cols] = (master / peak).astype(BF16)
        master_out[:, cols] = master
        first_out[:, cols] = first
        second_out[:, cols] = second
        peaks.append(peak)
    scales_ref[...] = jnp.concatenate(peaks, axis=1)


def update(own, left, right, master, first, second):
    rows, width = master.shape
    tile = min(128, rows)
    spec = pl.BlockSpec((tile, width), lambda i: (i, 0))
    blocks = width // BLK
    return pl.pallas_call(
        update_kernel,
        out_shape=(
            jax.ShapeDtypeStruct((rows, width), BF16),
            jax.ShapeDtypeStruct((rows, blocks), F32),
            jax.ShapeDtypeStruct((rows, width), F32),
            jax.ShapeDtypeStruct((rows, width), F32),
            jax.ShapeDtypeStruct((rows, width), F32),
        ),
        grid=(rows // tile,),
        in_specs=[spec] * 6,
        out_specs=(spec, pl.BlockSpec((tile, blocks), lambda i: (i, 0)), spec, spec, spec),
        compiler_params=pltpu.CompilerParams(vmem_limit_bytes=32 * 1024 * 1024),
        name="update",
        cost_estimate=pl.CostEstimate(
            flops=20 * rows * width, bytes_accessed=32 * rows * width, transcendentals=rows * width
        ),
    )(own, left, right, master, first, second)


def shift(value, by):
    size = lax.axis_size("query")
    return lax.ppermute(value, "query", [(i, (i + by) % size) for i in range(size)])


def place(x, z, core):
    return (x % 4 * 4 + z % 4) * 2 + core


def hop(value, x=0, z=0, core=0):
    pairs = [
        (place(a, b, c), place(a + x, b + z, c ^ core))
        for a in range(4)
        for b in range(4)
        for c in range(2)
    ]
    return lax.ppermute(value, "cluster", pairs)


def add(*values):
    return sum(value.astype(F32) for value in values).astype(BF16)


def ring_open(b, c, send):
    return send(b, 1), send(c, -1)


def ring_close(own, a, d, left, right, send):
    half = a.shape[0]
    left_low = send(add(a, left[half:]), 1)
    right_high = send(add(d, right[:half]), -1)
    return (own, jnp.concatenate([left_low, left[:half]]), jnp.concatenate([right[half:], right_high]))


def ring_sum(value, send):
    own, a, b, c, d = cut(value)
    return add(*ring_close(own, a, d, *ring_open(b, c, send), send))


def cut(value):
    n = value.shape[0] // 4
    half = n // 2
    return value[:n], value[n : n + half], value[n + half : 2 * n + half], value[2 * n + half : 4 * n - half], value[4 * n - half :]


def ring_sum_small(value, send):
    n = value.shape[0] // 4
    parts = [send(value[j * n : (j + 1) * n], j if j < 3 else -1) for j in range(1, 4)]
    return add(value[:n], *parts)


def along_x(value, by):
    return hop(value, x=by)


def along_z(value, by):
    return hop(value, z=by)


def per_device(
    queries,
    positives,
    neg_clusters,
    owner_map,
    label_codes,
    label_scales,
    label_master,
    first_moment,
    second_moment,
):
    n_col, quarter, width = label_codes.shape
    crows = 4 * quarter
    half = n_col // 2
    my_y = lax.axis_index("query")
    my_col = lax.axis_index("cluster")

    own = dequantize(
        label_codes.reshape(n_col * quarter, width),
        label_scales.reshape(n_col * quarter, width // BLK),
    ).reshape(n_col, quarter, width)
    left, right = shift(own, 1), shift(own, -1)

    pair_ids = jnp.concatenate([neg_clusters, hop(neg_clusters, core=1)], axis=1)
    digits = jnp.concatenate([pair_ids // 64, pair_ids % 64], axis=1).astype(BF16)
    digits = jnp.pad(digits, ((0, ID_ROWS - 1), (0, width - digits.shape[1])))
    mine = jnp.concatenate([queries[0], digits])
    half_rows = mine.shape[0] // 2
    x_left, x_right = along_x(mine, 1), along_x(mine, -1)
    x_low, x_high = along_x(x_left[:half_rows], 1), along_x(x_right[half_rows:], -1)
    strip = jnp.stack([mine, x_right, jnp.concatenate([x_low, x_high]), x_left])
    z_left, z_right = along_z(strip, 1), along_z(strip, -1)
    far_low, far_high = shift(left[:half], 1), shift(right[half:], -1)
    z_low, z_high = along_z(z_left[:2], 1), along_z(z_right[2:], -1)
    pieces = (strip, z_right, z_left, z_low, z_high)
    pieces = pieces + (hop(strip, core=1),)
    pieces = pieces + (hop(z_right, core=1), hop(z_left, core=1))
    pieces = pieces + (hop(z_low, core=1), hop(z_high, core=1))
    digits = jnp.concatenate([piece[:, -ID_ROWS, :128] for piece in pieces[:5]]).astype(I32)
    group_ids = (digits[:, :64] * 64 + digits[:, 64:]).reshape(-1)

    places = my_col * n_col + jnp.arange(n_col, dtype=I32)
    all_ids = jnp.arange(owner_map.shape[0], dtype=I32)
    held = jnp.sum(jnp.where(owner_map[None, :] == places[:, None], all_ids[None, :], 0), axis=1)
    listed = jnp.sum((group_ids[None, :] == held[:, None]).astype(I32), axis=1)
    count = jnp.sum(listed)
    local = jnp.arange(n_col, dtype=I32)
    before = local[None, :] < local[:, None]
    ahead = jnp.sum(jnp.where(before, listed[None, :], 0), axis=1)
    rank = jnp.where(listed > 0, ahead, count + local - ahead)
    place = rank[None, :] == local[:, None]
    order = jnp.sum(jnp.where(place, local[None, :], 0), axis=1)
    base = jnp.sum(jnp.where(place, held[None, :], 0), axis=1) * crows
    info = jnp.stack([count, my_y.astype(I32), my_col.astype(I32)])
    *query_parts, label_own, label_a, label_b, label_c, label_d = score_and_grads(
        order,
        base,
        info,
        positives.reshape(-1, 128),
        (own, right, left, far_low, far_high),
        pieces,
    )
    label_hops = ring_open(label_b, label_c, shift)
    mine_u, mine_v, part_u, part_v = query_parts
    u = add(mine_u, hop(part_u, core=1))
    v = add(mine_v, hop(part_v, core=1))
    u = ring_sum(u, along_x)
    v = ring_sum(v, along_z)
    label_left, label_right, u, v = lax.optimization_barrier((*label_hops, u, v))
    label_parts = ring_close(label_own, label_a, label_d, label_left, label_right, shift)
    u = ring_sum_small(u, along_z)
    v = ring_sum_small(v, along_x)
    query_grad = jnp.concatenate([u[0], v[0]]).astype(F32)

    flat = lambda value: value.reshape(n_col * quarter, width)
    new_codes, new_scales, new_master, new_first, new_second = update(
        *(flat(part) for part in label_parts),
        flat(label_master),
        flat(first_moment),
        flat(second_moment),
    )
    shape = label_master.shape
    return (
        query_grad[None],
        new_codes.reshape(shape),
        new_scales.reshape(n_col, quarter, width // BLK),
        new_master.reshape(shape),
        new_first.reshape(shape),
        new_second.reshape(shape),
    )


def solution(mesh):
    in_specs = (
        P("query", "cluster", None),
        P("query", None),
        P("query", "cluster"),
        P(),
        P("cluster", "query", None),
        P("cluster", "query", None),
        P("cluster", "query", None),
        P("cluster", "query", None),
        P("cluster", "query", None),
    )
    out_specs = (
        P("query", "cluster", None),
        P("cluster", "query", None),
        P("cluster", "query", None),
        P("cluster", "query", None),
        P("cluster", "query", None),
        P("cluster", "query", None),
    )

    return jax.shard_map(
        per_device, mesh=mesh, in_specs=in_specs, out_specs=out_specs, check_vma=False
    )
```

```python
import math

import jax
import jax.numpy as jnp
from jax import lax
from jax.experimental import pallas as pl
from jax.experimental.pallas import tpu as pltpu
from jax.sharding import PartitionSpec as P


BLK = 128

pos_weight = 64.0
beta_first = 0.9
beta_second = 0.95
learn_rate = 0.05
adam_eps = 1e-08
adam_step = 20.0
scale_eps = 1e-06

STEP = 4
SUB = 512
SPLIT1, SPLIT2, SPLIT3 = 1,1,1

F32, BF16, I32 = jnp.float32, jnp.bfloat16, jnp.int32
ANY = pl.BlockSpec(memory_space=pl.ANY)
VMEM_LIMIT = 62 * 1024 * 1024


def dequant_kernel(codes_ref, scales_ref, rows_ref):
    n_col, quarter, width = codes_ref.shape
    for col in range(n_col):
        for blk in range(width // BLK):
            cols = slice(blk * BLK, (blk + 1) * BLK)
            scale = jnp.broadcast_to(scales_ref[blk, :, col : col + 1], (quarter, BLK))
            rows_ref[col, :, cols] = (codes_ref[col, :, cols].astype(F32) * scale).astype(BF16)


def dequantize(codes, scales):
    whole = pl.BlockSpec(memory_space=pltpu.VMEM)
    return pl.pallas_call(
        dequant_kernel,
        out_shape=jax.ShapeDtypeStruct(codes.shape, BF16),
        in_specs=[whole, whole],
        out_specs=whole,
        name="dequantize",
        cost_estimate=pl.CostEstimate(
            flops=codes.size, bytes_accessed=4 * codes.size, transcendentals=0
        ),
    )(codes, scales)


def score_kernel(
    order_ref, base_ref, info_ref, pid_hbm, own_hbm, right_hbm, left_hbm, low_hbm, high_hbm, *refs
):
    q_pieces, refs = (refs[:5], refs[5:10]), refs[10:]
    mine_u, mine_v, part_u, part_v, lab_own, lab_a, lab_b, lab_c, lab_d = refs[:9]
    q_ref, qt_ref, ids_ref, pid_ref, w_ref, acc_ref, wb_ref, id_ref, sa_ref, sb_ref = refs[9:19]
    pa_ref, pb_ref, lt_ref, lab_ref, qg_ref, sem, q_sem, lab_sem, out_sem = refs[19:]
    total, width = q_ref.shape
    n_col, quarter = w_ref.shape[0] // 4, w_ref.shape[1]
    half = n_col // 2
    crows = 4 * quarter
    rows = STEP * crows
    n_pair = total // (2 * SUB)
    inv_root = 1.0 / math.sqrt(width)
    power_scale = math.log2(math.e) * inv_root
    listed = info_ref[0]
    my_y = info_ref[1]
    n_block = lax.div(listed + STEP - 1, STEP)

    def rows_of(start, size):
        return pl.ds(pl.multiple_of(start, size), size)

    my_col = info_ref[2]
    my_x, my_z, my_core = lax.div(my_col, 8), lax.rem(lax.div(my_col, 2), 4), lax.rem(my_col, 2)
    share = total // 32

    load_q = []
    for core in range(2):
        own_q, right_q, left_q, low_q, high_q = q_pieces[core]
        for z, x in ((z, x) for z in range(4) for x in range(4)):
            src = (own_q, right_q, (low_q, high_q)[x // 2], left_q)[z].at[x % 2 if z == 2 else x]
            col = (lax.rem(my_x + x, 4) * 4 + lax.rem(my_z + z, 4)) * 2
            col = col + (my_core if core == 0 else 1 - my_core)
            load_q.append(
                pltpu.make_async_copy(
                    src.at[pl.ds(0, share)], q_ref.at[rows_of(col * share, share)], q_sem.at[col]
                )
            )
    targets = ((0, n_col), (n_col, n_col), (3 * n_col, n_col), (2 * n_col, half), (2 * n_col + half, half))
    pieces = (own_hbm, right_hbm, left_hbm, low_hbm, high_hbm)
    loads = [
        pltpu.make_async_copy(src, w_ref.at[pl.ds(*at)], sem.at[i])
        for i, (src, at) in enumerate(zip(pieces, targets, strict=True))
    ]
    load_ids = pltpu.make_async_copy(pid_hbm, ids_ref, sem.at[5])
    load_ids.start()
    for copy in load_q + loads:
        copy.start()

    def clear(entry, carry):
        where = order_ref[entry]
        for j in range(4):
            lab_ref[j * n_col + where] = jnp.zeros((quarter, width), BF16)
        return carry

    lax.fori_loop(listed, n_col, clear, 0)

    load_ids.wait()

    def spread(i, carry):
        row = jnp.broadcast_to(ids_ref[pl.ds(i, 1), :], (128, 128))
        pid_ref[rows_of(i * 128, 128), :] = row.T
        return carry

    lax.fori_loop(0, total // 128, spread, 0)

    def flip(i, carry):
        for h in range(2):
            k = 2 * i + h
            pltpu.make_async_copy(
                q_pieces[0][0].at[0, pl.ds(0, share)], q_ref.at[rows_of(k * share, share)], q_sem.at[k]
            ).wait()
        at = rows_of(i * 2 * share, 2 * share)
        qt_ref[:, at] = q_ref[at, :].T
        return carry

    lax.fori_loop(0, 16, flip, 0)

    for copy in loads:
        copy.wait()

    lane = lax.broadcasted_iota(I32, (8, rows), 1)
    slot = lax.div(lane, jnp.full_like(lane, crows))
    within = lax.rem(lane, jnp.full_like(lane, crows))
    part = lax.rem(lax.div(within, jnp.full_like(lane, quarter)) + my_y, jnp.full_like(lane, 4))
    row_id = part * quarter + lax.rem(within, jnp.full_like(lane, quarter))

    def stage(block):
        buf = lax.rem(block, 2)
        ids = row_id
        for k in range(STEP):
            entry = jnp.minimum(block * STEP + k, n_col - 1)
            valid = block * STEP + k < listed
            where = order_ref[entry]
            ids = ids + jnp.where(slot == k, base_ref[entry], 0)
            for j in range(4):
                start = k * crows + j * quarter
                held = w_ref[j * n_col + where]
                wb_ref[buf, start : start + quarter, :] = jnp.where(
                    valid, held, jnp.zeros_like(held)
                )
        id_ref[buf] = ids

    def score(block, start, to_ref):
        size = SUB // SPLIT1
        for h in range(SPLIT1):
            to_ref[h * size : (h + 1) * size] = lax.dot_general(
                q_ref[rows_of(start + h * size, size), :],
                wb_ref[lax.rem(block, 2)],
                (((1,), (1,)), ((), ())),
                preferred_element_type=F32,
            )

    def slopes(block, start, from_ref, to_ref):
        pid = pid_ref[rows_of(start, SUB), :]
        ids = id_ref[lax.rem(block, 2)]
        for c in range(rows // 128):
            cols = slice(c * 128, (c + 1) * 128)
            hit = pid == ids[0:1, cols]
            power = from_ref[:, cols] * jnp.where(hit, power_scale, -power_scale)
            prob = jnp.where(hit, -pos_weight, 1.0) / (1.0 + jnp.exp2(power))
            to_ref[:, cols] = prob.astype(BF16)

    def grads(block, start, p_ref, lt_is_new):
        size = SUB // SPLIT2
        for h in range(SPLIT2):
            at = rows_of(start + h * size, size)
            old = jnp.where(block == 0, 0.0, acc_ref[at, :])
            acc_ref[at, :] = old + jnp.dot(
                p_ref[h * size : (h + 1) * size],
                wb_ref[lax.rem(block, 2)],
                preferred_element_type=F32,
            )
        buf = lax.rem(block, 2)
        size = width // SPLIT3
        for h in range(SPLIT3):
            cols = slice(h * size, (h + 1) * size)
            old = jnp.where(lt_is_new, 0.0, lt_ref[buf, cols])
            lt_ref[buf, cols] = old + jnp.dot(
                qt_ref[cols, rows_of(start, SUB)], p_ref[...], preferred_element_type=F32
            )

    def emit(block):
        lab = (lt_ref[lax.rem(block, 2)] * inv_root).T
        for k in range(STEP):
            entry = block * STEP + k

            @pl.when(entry < listed)
            def _(k=k, entry=entry):
                where = order_ref[entry]
                for j in range(4):
                    start = k * crows + j * quarter
                    lab_ref[j * n_col + where] = lab[start : start + quarter, :].astype(BF16)

    @pl.when(n_block > 0)
    def _():
        stage(0)
        score(0, 0, sa_ref)
        pb_ref[...] = jnp.zeros_like(pb_ref)

    def pair(t, carry):
        block, at = lax.div(t, n_pair), lax.rem(t, n_pair)
        before = jnp.maximum(t - 1, 0)
        pblock, pat = lax.div(before, n_pair), lax.rem(before, n_pair)
        nblock, nat = lax.div(t + 1, n_pair), lax.rem(t + 1, n_pair)
        here = at * (2 * SUB)

        @pl.when(nat == 0)
        def _():
            stage(nblock)

        @pl.when((at == 1) & (block > 0))
        def _():
            emit(block - 1)

        slopes(block, here, sa_ref, pa_ref)
        score(block, here + SUB, sb_ref)
        grads(pblock, pat * (2 * SUB) + SUB, pb_ref, False)
        slopes(block, here + SUB, sb_ref, pb_ref)
        score(nblock, nat * (2 * SUB), sa_ref)
        grads(block, here, pa_ref, at == 0)
        return carry

    lax.fori_loop(0, n_block * n_pair, pair, 0)

    @pl.when(n_block > 0)
    def _():
        grads(n_block - 1, total - SUB, pb_ref, False)
        emit(n_block - 1)

    put_lab = []
    at = 0
    for i, out in enumerate((lab_own, lab_a, lab_b, lab_c, lab_d)):
        size = out.shape[0]
        put_lab.append(pltpu.make_async_copy(lab_ref.at[pl.ds(at, size)], out, lab_sem.at[i]))
        put_lab[-1].start()
        at += size

    part_rows = share // 2

    def puts(k, out_u, out_v):
        x, z = lax.rem(lax.div(k, 8) + 4 - my_x, 4), lax.rem(lax.div(k, 2) + 8 - my_z, 4)
        return (
            pltpu.make_async_copy(
                qg_ref.at[rows_of(k * share, part_rows)], out_u.at[x * 4 + z], out_sem.at[0, k]
            ),
            pltpu.make_async_copy(
                qg_ref.at[rows_of(k * share + part_rows, part_rows)],
                out_v.at[z * 4 + x],
                out_sem.at[1, k],
            ),
        )

    def finish(k, carry):
        at = rows_of(k * share, share)
        qg_ref[at, :] = jnp.where(n_block > 0, acc_ref[at, :] * inv_root, 0.0).astype(BF16)

        @pl.when(lax.rem(k, 2) == my_core)
        def _():
            for copy in puts(k, mine_u, mine_v):
                copy.start()

        @pl.when(lax.rem(k, 2) != my_core)
        def _():
            for copy in puts(k, part_u, part_v):
                copy.start()

        return carry

    lax.fori_loop(0, 32, finish, 0)

    def settle(k, carry):
        for copy in puts(k, mine_u, mine_v):
            copy.wait()
        return carry

    lax.fori_loop(0, 32, settle, 0)
    for copy in put_lab:
        copy.wait()


def score_and_grads(order, base, info, pid, quarters, queries):
    total, width = pid.size, quarters[0].shape[2]
    n_col, quarter = quarters[0].shape[0], quarters[0].shape[1]
    half = n_col // 2
    block = STEP * 4 * quarter
    smem = pl.BlockSpec(memory_space=pltpu.SMEM)
    share = jax.ShapeDtypeStruct((16, total // 64, width), BF16)
    label = lambda size: jax.ShapeDtypeStruct((size, quarter, width), BF16)
    return pl.pallas_call(
        score_kernel,
        out_shape=(share,) * 4
        + (label(n_col), label(half), label(n_col), label(n_col), label(half)),
        in_specs=[smem] * 3 + [ANY] * 16,
        out_specs=(ANY,) * 9,
        scratch_shapes=[
            pltpu.VMEM((total, width), BF16),
            pltpu.VMEM((width, total), BF16),
            pltpu.VMEM((total // 128, 128), I32),
            pltpu.VMEM((total, 128), I32),
            pltpu.VMEM((4 * n_col, quarter, width), BF16),
            pltpu.VMEM((total, width), F32),
            pltpu.VMEM((2, block, width), BF16),
            pltpu.VMEM((2, 8, block), I32),
            pltpu.VMEM((SUB, block), F32),
            pltpu.VMEM((SUB, block), F32),
            pltpu.VMEM((SUB, block), BF16),
            pltpu.VMEM((SUB, block), BF16),
            pltpu.VMEM((2, width, block), F32),
            pltpu.VMEM((4 * n_col, quarter, width), BF16),
            pltpu.VMEM((total, width), BF16),
            pltpu.SemaphoreType.DMA((6,)),
            pltpu.SemaphoreType.DMA((32,)),
            pltpu.SemaphoreType.DMA((5,)),
            pltpu.SemaphoreType.DMA((2, 32)),
        ],
        compiler_params=pltpu.CompilerParams(vmem_limit_bytes=VMEM_LIMIT),
        name="score",
        cost_estimate=pl.CostEstimate(
            flops=3 * total * n_col * 2 * quarter * width * 2,
            bytes_accessed=4 * total * width + 16 * n_col * quarter * width,
            transcendentals=total * n_col * 4 * quarter,
        ),
    )(order, base, info, pid, *quarters, *queries)


def update_kernel(
    own_ref, left_ref, right_ref, master_ref, first_ref, second_ref,
    codes_ref, scales_ref, master_out, first_out, second_out,
):
    width = master_ref.shape[1]
    fix_first = 1.0 - beta_first**adam_step
    fix_second = 1.0 - beta_second**adam_step
    peaks = []
    for blk in range(width // BLK):
        cols = slice(blk * BLK, (blk + 1) * BLK)
        grad = (
            own_ref[:, cols].astype(F32)
            + left_ref[:, cols].astype(F32)
            + right_ref[:, cols].astype(F32)
        )
        first = beta_first * first_ref[:, cols] + (1.0 - beta_first) * grad
        second = beta_second * second_ref[:, cols] + (1.0 - beta_second) * grad * grad
        master = master_ref[:, cols] - learn_rate * (first / fix_first) / (
            jnp.sqrt(second / fix_second) + adam_eps
        )
        peak = jnp.max(jnp.abs(master), axis=1, keepdims=True) + scale_eps
        codes_ref[:, cols] = (master / peak).astype(BF16)
        master_out[:, cols] = master
        first_out[:, cols] = first
        second_out[:, cols] = second
        peaks.append(peak)
    scales_ref[...] = jnp.concatenate(peaks, axis=1)


def update(own, left, right, master, first, second):
    rows, width = master.shape
    tile = min(128, rows)
    spec = pl.BlockSpec((tile, width), lambda i: (i, 0))
    blocks = width // BLK
    return pl.pallas_call(
        update_kernel,
        out_shape=(
            jax.ShapeDtypeStruct((rows, width), BF16),
            jax.ShapeDtypeStruct((rows, blocks), F32),
            jax.ShapeDtypeStruct((rows, width), F32),
            jax.ShapeDtypeStruct((rows, width), F32),
            jax.ShapeDtypeStruct((rows, width), F32),
        ),
        grid=(rows // tile,),
        in_specs=[spec] * 6,
        out_specs=(spec, pl.BlockSpec((tile, blocks), lambda i: (i, 0)), spec, spec, spec),
        compiler_params=pltpu.CompilerParams(vmem_limit_bytes=32 * 1024 * 1024),
        name="update",
        cost_estimate=pl.CostEstimate(
            flops=20 * rows * width, bytes_accessed=32 * rows * width, transcendentals=rows * width
        ),
    )(own, left, right, master, first, second)


def shift(value, by):
    size = lax.axis_size("query")
    return lax.ppermute(value, "query", [(i, (i + by) % size) for i in range(size)])


def place(x, z, core):
    return (x % 4 * 4 + z % 4) * 2 + core


def hop(value, x=0, z=0, core=0):
    pairs = [
        (place(a, b, c), place(a + x, b + z, c ^ core))
        for a in range(4)
        for b in range(4)
        for c in range(2)
    ]
    return lax.ppermute(value, "cluster", pairs)


def add(*values):
    return sum(value.astype(F32) for value in values).astype(BF16)


def ring_open(b, c, send):
    return send(b, 1), send(c, -1)


def ring_close(own, a, d, left, right, send):
    half = a.shape[0]
    left_low = send(add(a, left[half:]), 1)
    right_high = send(add(d, right[:half]), -1)
    return (own, jnp.concatenate([left_low, left[:half]]), jnp.concatenate([right[half:], right_high]))


def ring_sum(value, send):
    own, a, b, c, d = cut(value)
    return add(*ring_close(own, a, d, *ring_open(b, c, send), send))


def cut(value):
    n = value.shape[0] // 4
    half = n // 2
    return value[:n], value[n : n + half], value[n + half : 2 * n + half], value[2 * n + half : 4 * n - half], value[4 * n - half :]


def ring_sum_small(value, send):
    n = value.shape[0] // 4
    parts = [send(value[j * n : (j + 1) * n], j if j < 3 else -1) for j in range(1, 4)]
    return add(value[:n], *parts)


def along_x(value, by):
    return hop(value, x=by)


def along_z(value, by):
    return hop(value, z=by)


def per_device(
    queries,
    positives,
    neg_clusters,
    owner_map,
    label_codes,
    label_scales,
    label_master,
    first_moment,
    second_moment,
):
    n_col, quarter, width = label_codes.shape
    crows = 4 * quarter
    half = n_col // 2
    my_y = lax.axis_index("query")
    my_col = lax.axis_index("cluster")

    own = dequantize(label_codes, label_scales.transpose(2, 1, 0))
    left, right = shift(own, 1), shift(own, -1)

    mine = queries[0]
    half_rows = mine.shape[0] // 2
    x_left, x_right = along_x(mine, 1), along_x(mine, -1)
    x_low, x_high = along_x(x_left[:half_rows], 1), along_x(x_right[half_rows:], -1)
    strip = jnp.stack([mine, x_right, jnp.concatenate([x_low, x_high]), x_left])
    z_left, z_right = along_z(strip, 1), along_z(strip, -1)
    far_low, far_high = shift(left[:half], 1), shift(right[half:], -1)
    z_low, z_high = along_z(z_left[:2], 1), along_z(z_right[2:], -1)
    pieces = (strip, z_right, z_left, z_low, z_high)
    pieces = pieces + (hop(strip, core=1),)
    pieces = pieces + (hop(z_right, core=1), hop(z_left, core=1))
    pieces = pieces + (hop(z_low, core=1), hop(z_high, core=1))
    ids = jnp.concatenate([neg_clusters, hop(neg_clusters, core=1)], axis=1)
    ids = jnp.concatenate([ids] + [along_x(ids, by) for by in (1, -1, 2)])
    ids = jnp.concatenate([ids] + [along_z(ids, by) for by in (1, -1, 2)])
    group_ids = ids.reshape(-1)

    places = my_col * n_col + jnp.arange(n_col, dtype=I32)
    all_ids = jnp.arange(owner_map.shape[0], dtype=I32)
    held = jnp.sum(jnp.where(owner_map[None, :] == places[:, None], all_ids[None, :], 0), axis=1)
    listed = jnp.sum((group_ids[None, :] == held[:, None]).astype(I32), axis=1)
    count = jnp.sum(listed)
    local = jnp.arange(n_col, dtype=I32)
    before = local[None, :] < local[:, None]
    ahead = jnp.sum(jnp.where(before, listed[None, :], 0), axis=1)
    rank = jnp.where(listed > 0, ahead, count + local - ahead)
    place = rank[None, :] == local[:, None]
    order = jnp.sum(jnp.where(place, local[None, :], 0), axis=1)
    base = jnp.sum(jnp.where(place, held[None, :], 0), axis=1) * crows
    info = jnp.stack([count, my_y.astype(I32), my_col.astype(I32)])
    *query_parts, label_own, label_a, label_b, label_c, label_d = score_and_grads(
        order,
        base,
        info,
        positives.reshape(-1, 128),
        (own, right, left, far_low, far_high),
        pieces,
    )
    label_hops = ring_open(label_b, label_c, shift)
    mine_u, mine_v, part_u, part_v = query_parts
    u = add(mine_u, hop(part_u, core=1))
    v = add(mine_v, hop(part_v, core=1))
    u = ring_sum(u, along_x)
    v = ring_sum(v, along_z)
    label_left, label_right, u, v = lax.optimization_barrier((*label_hops, u, v))
    label_parts = ring_close(label_own, label_a, label_d, label_left, label_right, shift)
    u = ring_sum_small(u, along_z)
    v = ring_sum_small(v, along_x)
    query_grad = jnp.concatenate([u[0], v[0]]).astype(F32)

    flat = lambda value: value.reshape(n_col * quarter, width)
    new_codes, new_scales, new_master, new_first, new_second = update(
        *(flat(part) for part in label_parts),
        flat(label_master),
        flat(first_moment),
        flat(second_moment),
    )
    shape = label_master.shape
    return (
        query_grad[None],
        new_codes.reshape(shape),
        new_scales.reshape(n_col, quarter, width // BLK),
        new_master.reshape(shape),
        new_first.reshape(shape),
        new_second.reshape(shape),
    )


def solution(mesh):
    in_specs = (
        P("query", "cluster", None),
        P("query", None),
        P("query", "cluster"),
        P(),
        P("cluster", "query", None),
        P("cluster", "query", None),
        P("cluster", "query", None),
        P("cluster", "query", None),
        P("cluster", "query", None),
    )
    out_specs = (
        P("query", "cluster", None),
        P("cluster", "query", None),
        P("cluster", "query", None),
        P("cluster", "query", None),
        P("cluster", "query", None),
        P("cluster", "query", None),
    )

    return jax.shard_map(
        per_device, mesh=mesh, in_specs=in_specs, out_specs=out_specs, check_vma=False
    )
```

```python
import math

import jax
import jax.numpy as jnp
from jax import lax
from jax.experimental import pallas as pl
from jax.experimental.pallas import tpu as pltpu
from jax.sharding import PartitionSpec as P


BLK = 128

pos_weight = 64.0
beta_first = 0.9
beta_second = 0.95
learn_rate = 0.05
adam_eps = 1e-08
adam_step = 20.0
scale_eps = 1e-06

STEP = 4
SUB = 512
SPLIT1, SPLIT2, SPLIT3 = 1,1,1

F32, BF16, I32 = jnp.float32, jnp.bfloat16, jnp.int32
ANY = pl.BlockSpec(memory_space=pl.ANY)
VMEM_LIMIT = 62 * 1024 * 1024


def dequant_kernel(codes_ref, scales_ref, rows_ref):
    n_col, quarter, width = codes_ref.shape
    for col in range(n_col):
        for blk in range(width // BLK):
            cols = slice(blk * BLK, (blk + 1) * BLK)
            scale = jnp.broadcast_to(scales_ref[blk, :, col : col + 1], (quarter, BLK))
            rows_ref[col, :, cols] = (codes_ref[col, :, cols].astype(F32) * scale).astype(BF16)


def dequantize(codes, scales):
    whole = pl.BlockSpec(memory_space=pltpu.VMEM)
    return pl.pallas_call(
        dequant_kernel,
        out_shape=jax.ShapeDtypeStruct(codes.shape, BF16),
        in_specs=[whole, whole],
        out_specs=whole,
        name="dequantize",
        cost_estimate=pl.CostEstimate(
            flops=codes.size, bytes_accessed=4 * codes.size, transcendentals=0
        ),
    )(codes, scales)


def score_kernel(
    order_ref, base_ref, info_ref, pid_hbm, own_hbm, right_hbm, left_hbm, low_hbm, high_hbm, *refs
):
    q_pieces, refs = (refs[:5], refs[5:10]), refs[10:]
    mine_u, mine_v, part_u, part_v, lab_own, lab_a, lab_b, lab_c, lab_d = refs[:9]
    q_ref, qt_ref, ids_ref, pid_ref, w_ref, acc_ref, wb_ref, id_ref, sa_ref, sb_ref = refs[9:19]
    pa_ref, pb_ref, lt_ref, lab_ref, qg_ref, sem, q_sem, lab_sem, out_sem = refs[19:]
    total, width = q_ref.shape
    n_col, quarter = w_ref.shape[0] // 4, w_ref.shape[1]
    half = n_col // 2
    crows = 4 * quarter
    rows = STEP * crows
    n_pair = total // (2 * SUB)
    inv_root = 1.0 / math.sqrt(width)
    power_scale = math.log2(math.e) * inv_root
    listed = info_ref[0]
    my_y = info_ref[1]
    n_block = lax.div(listed + STEP - 1, STEP)

    def rows_of(start, size):
        return pl.ds(pl.multiple_of(start, size), size)

    my_col = info_ref[2]
    my_x, my_z, my_core = lax.div(my_col, 8), lax.rem(lax.div(my_col, 2), 4), lax.rem(my_col, 2)
    share = total // 32

    load_q = []
    for core in range(2):
        own_q, right_q, left_q, low_q, high_q = q_pieces[core]
        for z, x in ((z, x) for z in range(4) for x in range(4)):
            src = (own_q, right_q, (low_q, high_q)[x // 2], left_q)[z].at[x % 2 if z == 2 else x]
            col = (lax.rem(my_x + x, 4) * 4 + lax.rem(my_z + z, 4)) * 2
            col = col + (my_core if core == 0 else 1 - my_core)
            load_q.append(
                pltpu.make_async_copy(
                    src.at[pl.ds(0, share)], q_ref.at[rows_of(col * share, share)], q_sem.at[col]
                )
            )
    targets = ((0, n_col), (n_col, n_col), (3 * n_col, n_col), (2 * n_col, half), (2 * n_col + half, half))
    pieces = (own_hbm, right_hbm, left_hbm, low_hbm, high_hbm)
    loads = [
        pltpu.make_async_copy(src, w_ref.at[pl.ds(*at)], sem.at[i])
        for i, (src, at) in enumerate(zip(pieces, targets, strict=True))
    ]
    load_ids = pltpu.make_async_copy(pid_hbm, ids_ref, sem.at[5])
    load_ids.start()
    for copy in load_q + loads:
        copy.start()

    def clear(entry, carry):
        where = order_ref[entry]
        for j in range(4):
            lab_ref[j * n_col + where] = jnp.zeros((quarter, width), BF16)
        return carry

    lax.fori_loop(listed, n_col, clear, 0)

    load_ids.wait()

    def spread(i, carry):
        row = jnp.broadcast_to(ids_ref[pl.ds(i, 1), :], (128, 128))
        pid_ref[rows_of(i * 128, 128), :] = row.T
        return carry

    lax.fori_loop(0, total // 128, spread, 0)

    def flip(i, carry):
        for h in range(2):
            k = 2 * i + h
            pltpu.make_async_copy(
                q_pieces[0][0].at[0, pl.ds(0, share)], q_ref.at[rows_of(k * share, share)], q_sem.at[k]
            ).wait()
        at = rows_of(i * 2 * share, 2 * share)
        qt_ref[:, at] = q_ref[at, :].T
        return carry

    lax.fori_loop(0, 16, flip, 0)

    for copy in loads:
        copy.wait()

    lane = lax.broadcasted_iota(I32, (8, rows), 1)
    slot = lax.div(lane, jnp.full_like(lane, crows))
    within = lax.rem(lane, jnp.full_like(lane, crows))
    part = lax.rem(lax.div(within, jnp.full_like(lane, quarter)) + my_y, jnp.full_like(lane, 4))
    row_id = part * quarter + lax.rem(within, jnp.full_like(lane, quarter))

    def stage(block):
        buf = lax.rem(block, 2)
        ids = row_id
        for k in range(STEP):
            entry = jnp.minimum(block * STEP + k, n_col - 1)
            valid = block * STEP + k < listed
            where = order_ref[entry]
            ids = ids + jnp.where(slot == k, base_ref[entry], 0)
            for j in range(4):
                start = k * crows + j * quarter
                held = w_ref[j * n_col + where]
                wb_ref[buf, start : start + quarter, :] = jnp.where(
                    valid, held, jnp.zeros_like(held)
                )
        id_ref[buf] = ids

    def score(block, start, to_ref):
        size = SUB // SPLIT1
        for h in range(SPLIT1):
            to_ref[h * size : (h + 1) * size] = lax.dot_general(
                q_ref[rows_of(start + h * size, size), :],
                wb_ref[lax.rem(block, 2)],
                (((1,), (1,)), ((), ())),
                preferred_element_type=F32,
            )

    def slopes(block, start, from_ref, to_ref):
        pid = pid_ref[rows_of(start, SUB), :]
        ids = id_ref[lax.rem(block, 2)]
        for c in range(rows // 128):
            cols = slice(c * 128, (c + 1) * 128)
            hit = pid == ids[0:1, cols]
            power = from_ref[:, cols] * jnp.where(hit, power_scale, -power_scale)
            prob = jnp.where(hit, -pos_weight, 1.0) / (1.0 + jnp.exp2(power))
            to_ref[:, cols] = prob.astype(BF16)

    def grads(block, start, p_ref, lt_is_new):
        size = SUB // SPLIT2
        for h in range(SPLIT2):
            at = rows_of(start + h * size, size)
            old = jnp.where(block == 0, 0.0, acc_ref[at, :])
            acc_ref[at, :] = old + jnp.dot(
                p_ref[h * size : (h + 1) * size],
                wb_ref[lax.rem(block, 2)],
                preferred_element_type=F32,
            )
        buf = lax.rem(block, 2)
        size = width // SPLIT3
        for h in range(SPLIT3):
            cols = slice(h * size, (h + 1) * size)
            old = jnp.where(lt_is_new, 0.0, lt_ref[buf, cols])
            lt_ref[buf, cols] = old + jnp.dot(
                qt_ref[cols, rows_of(start, SUB)], p_ref[...], preferred_element_type=F32
            )

    def emit(block):
        lab = (lt_ref[lax.rem(block, 2)] * inv_root).T
        for k in range(STEP):
            entry = block * STEP + k

            @pl.when(entry < listed)
            def _(k=k, entry=entry):
                where = order_ref[entry]
                for j in range(4):
                    start = k * crows + j * quarter
                    lab_ref[j * n_col + where] = lab[start : start + quarter, :].astype(BF16)

    @pl.when(n_block > 0)
    def _():
        stage(0)
        score(0, 0, sa_ref)
        pb_ref[...] = jnp.zeros_like(pb_ref)

    def pair(t, carry):
        block, at = lax.div(t, n_pair), lax.rem(t, n_pair)
        before = jnp.maximum(t - 1, 0)
        pblock, pat = lax.div(before, n_pair), lax.rem(before, n_pair)
        nblock, nat = lax.div(t + 1, n_pair), lax.rem(t + 1, n_pair)
        here = at * (2 * SUB)

        @pl.when(nat == 0)
        def _():
            stage(nblock)

        @pl.when((at == 1) & (block > 0))
        def _():
            emit(block - 1)

        slopes(block, here, sa_ref, pa_ref)
        score(block, here + SUB, sb_ref)
        grads(pblock, pat * (2 * SUB) + SUB, pb_ref, False)
        slopes(block, here + SUB, sb_ref, pb_ref)
        score(nblock, nat * (2 * SUB), sa_ref)
        grads(block, here, pa_ref, at == 0)
        return carry

    lax.fori_loop(0, n_block * n_pair, pair, 0)

    @pl.when(n_block > 0)
    def _():
        grads(n_block - 1, total - SUB, pb_ref, False)
        emit(n_block - 1)

    put_lab = []
    at = 0
    for i, out in enumerate((lab_own, lab_a, lab_b, lab_c, lab_d)):
        size = out.shape[0]
        put_lab.append(pltpu.make_async_copy(lab_ref.at[pl.ds(at, size)], out, lab_sem.at[i]))
        put_lab[-1].start()
        at += size

    part_rows = share // 2

    def puts(k, out_u, out_v):
        x, z = lax.rem(lax.div(k, 8) + 4 - my_x, 4), lax.rem(lax.div(k, 2) + 8 - my_z, 4)
        return (
            pltpu.make_async_copy(
                qg_ref.at[rows_of(k * share, part_rows)], out_u.at[x * 4 + z], out_sem.at[0, k]
            ),
            pltpu.make_async_copy(
                qg_ref.at[rows_of(k * share + part_rows, part_rows)],
                out_v.at[z * 4 + x],
                out_sem.at[1, k],
            ),
        )

    def finish(k, carry):
        at = rows_of(k * share, share)
        qg_ref[at, :] = jnp.where(n_block > 0, acc_ref[at, :] * inv_root, 0.0).astype(BF16)

        @pl.when(lax.rem(k, 2) == my_core)
        def _():
            for copy in puts(k, mine_u, mine_v):
                copy.start()

        @pl.when(lax.rem(k, 2) != my_core)
        def _():
            for copy in puts(k, part_u, part_v):
                copy.start()

        return carry

    lax.fori_loop(0, 32, finish, 0)

    def settle(k, carry):
        for copy in puts(k, mine_u, mine_v):
            copy.wait()
        return carry

    lax.fori_loop(0, 32, settle, 0)
    for copy in put_lab:
        copy.wait()


def score_and_grads(order, base, info, pid, quarters, queries):
    total, width = pid.size, quarters[0].shape[2]
    n_col, quarter = quarters[0].shape[0], quarters[0].shape[1]
    half = n_col // 2
    block = STEP * 4 * quarter
    smem = pl.BlockSpec(memory_space=pltpu.SMEM)
    share = jax.ShapeDtypeStruct((16, total // 64, width), BF16)
    label = lambda size: jax.ShapeDtypeStruct((size, quarter, width), BF16)
    return pl.pallas_call(
        score_kernel,
        out_shape=(share,) * 4
        + (label(n_col), label(half), label(n_col), label(n_col), label(half)),
        in_specs=[smem] * 3 + [ANY] * 16,
        out_specs=(ANY,) * 9,
        scratch_shapes=[
            pltpu.VMEM((total, width), BF16),
            pltpu.VMEM((width, total), BF16),
            pltpu.VMEM((total // 128, 128), I32),
            pltpu.VMEM((total, 128), I32),
            pltpu.VMEM((4 * n_col, quarter, width), BF16),
            pltpu.VMEM((total, width), F32),
            pltpu.VMEM((2, block, width), BF16),
            pltpu.VMEM((2, 8, block), I32),
            pltpu.VMEM((SUB, block), F32),
            pltpu.VMEM((SUB, block), F32),
            pltpu.VMEM((SUB, block), BF16),
            pltpu.VMEM((SUB, block), BF16),
            pltpu.VMEM((2, width, block), F32),
            pltpu.VMEM((4 * n_col, quarter, width), BF16),
            pltpu.VMEM((total, width), BF16),
            pltpu.SemaphoreType.DMA((6,)),
            pltpu.SemaphoreType.DMA((32,)),
            pltpu.SemaphoreType.DMA((5,)),
            pltpu.SemaphoreType.DMA((2, 32)),
        ],
        compiler_params=pltpu.CompilerParams(vmem_limit_bytes=VMEM_LIMIT),
        name="score",
        cost_estimate=pl.CostEstimate(
            flops=3 * total * n_col * 2 * quarter * width * 2,
            bytes_accessed=4 * total * width + 16 * n_col * quarter * width,
            transcendentals=total * n_col * 4 * quarter,
        ),
    )(order, base, info, pid, *quarters, *queries)


def update_kernel(
    own_ref, left_ref, right_ref, master_ref, first_ref, second_ref,
    codes_ref, scales_ref, master_out, first_out, second_out,
):
    width = master_ref.shape[1]
    fix_first = 1.0 - beta_first**adam_step
    fix_second = 1.0 - beta_second**adam_step
    peaks = []
    for blk in range(width // BLK):
        cols = slice(blk * BLK, (blk + 1) * BLK)
        grad = (
            own_ref[:, cols].astype(F32)
            + left_ref[:, cols].astype(F32)
            + right_ref[:, cols].astype(F32)
        )
        first = beta_first * first_ref[:, cols] + (1.0 - beta_first) * grad
        second = beta_second * second_ref[:, cols] + (1.0 - beta_second) * grad * grad
        master = master_ref[:, cols] - first * (learn_rate / fix_first) / (
            jnp.sqrt(second * (1.0 / fix_second)) + adam_eps
        )
        peak = jnp.max(jnp.abs(master), axis=1, keepdims=True) + scale_eps
        codes_ref[:, cols] = (master * (1.0 / peak)).astype(BF16)
        master_out[:, cols] = master
        first_out[:, cols] = first
        second_out[:, cols] = second
        peaks.append(peak)
    scales_ref[...] = jnp.concatenate(peaks, axis=1)


def update(own, left, right, master, first, second):
    rows, width = master.shape
    tile = min(128, rows)
    spec = pl.BlockSpec((tile, width), lambda i: (i, 0))
    blocks = width // BLK
    return pl.pallas_call(
        update_kernel,
        out_shape=(
            jax.ShapeDtypeStruct((rows, width), BF16),
            jax.ShapeDtypeStruct((rows, blocks), F32),
            jax.ShapeDtypeStruct((rows, width), F32),
            jax.ShapeDtypeStruct((rows, width), F32),
            jax.ShapeDtypeStruct((rows, width), F32),
        ),
        grid=(rows // tile,),
        in_specs=[spec] * 6,
        out_specs=(spec, pl.BlockSpec((tile, blocks), lambda i: (i, 0)), spec, spec, spec),
        compiler_params=pltpu.CompilerParams(vmem_limit_bytes=32 * 1024 * 1024),
        name="update",
        cost_estimate=pl.CostEstimate(
            flops=20 * rows * width, bytes_accessed=32 * rows * width, transcendentals=rows * width
        ),
    )(own, left, right, master, first, second)


def shift(value, by):
    size = lax.axis_size("query")
    return lax.ppermute(value, "query", [(i, (i + by) % size) for i in range(size)])


def place(x, z, core):
    return (x % 4 * 4 + z % 4) * 2 + core


def hop(value, x=0, z=0, core=0):
    pairs = [
        (place(a, b, c), place(a + x, b + z, c ^ core))
        for a in range(4)
        for b in range(4)
        for c in range(2)
    ]
    return lax.ppermute(value, "cluster", pairs)


def add(*values):
    return sum(value.astype(F32) for value in values).astype(BF16)


def ring_open(b, c, send):
    return send(b, 1), send(c, -1)


def ring_far(a, d, left, right):
    half = a.shape[0]
    return add(a, left[half:]), add(d, right[:half])


def ring_close(own, far, left, right, send):
    half = far[0].shape[0]
    left_low, right_high = send(far[0], 1), send(far[1], -1)
    return (own, jnp.concatenate([left_low, left[:half]]), jnp.concatenate([right[half:], right_high]))


def cut(value):
    n = value.shape[0] // 4
    half = n // 2
    return value[:n], value[n : n + half], value[n + half : 2 * n + half], value[2 * n + half : 4 * n - half], value[4 * n - half :]


def ring_sum_small(value, send):
    n = value.shape[0] // 4
    parts = [send(value[j * n : (j + 1) * n], j if j < 3 else -1) for j in range(1, 4)]
    return add(value[:n], *parts)


def along_x(value, by):
    return hop(value, x=by)


def along_z(value, by):
    return hop(value, z=by)


def per_device(
    queries,
    positives,
    neg_clusters,
    owner_map,
    label_codes,
    label_scales,
    label_master,
    first_moment,
    second_moment,
):
    n_col, quarter, width = label_codes.shape
    crows = 4 * quarter
    half = n_col // 2
    my_y = lax.axis_index("query")
    my_col = lax.axis_index("cluster")

    own = dequantize(label_codes, label_scales.transpose(2, 1, 0))
    left, right = shift(own, 1), shift(own, -1)

    mine = queries[0]
    half_rows = mine.shape[0] // 2
    x_left, x_right = along_x(mine, 1), along_x(mine, -1)
    x_low, x_high = along_x(x_left[:half_rows], 1), along_x(x_right[half_rows:], -1)
    strip = jnp.stack([mine, x_right, jnp.concatenate([x_low, x_high]), x_left])
    z_left, z_right = along_z(strip, 1), along_z(strip, -1)
    far_low, far_high = shift(left[:half], 1), shift(right[half:], -1)
    z_low, z_high = along_z(z_left[:2], 1), along_z(z_right[2:], -1)
    pieces = (strip, z_right, z_left, z_low, z_high)
    ids = jnp.concatenate([neg_clusters, hop(neg_clusters, core=1)], axis=1)
    ids = jnp.concatenate([ids] + [along_x(ids, by) for by in (1, -1, 2)])
    ids = jnp.concatenate([ids] + [along_z(ids, by) for by in (1, -1, 2)])
    group_ids = ids.reshape(-1)

    places = my_col * n_col + jnp.arange(n_col, dtype=I32)
    all_ids = jnp.arange(owner_map.shape[0], dtype=I32)
    held = jnp.sum(jnp.where(owner_map[None, :] == places[:, None], all_ids[None, :], 0), axis=1)
    listed = jnp.sum((group_ids[None, :] == held[:, None]).astype(I32), axis=1)
    count = jnp.sum(listed)
    local = jnp.arange(n_col, dtype=I32)
    before = local[None, :] < local[:, None]
    ahead = jnp.sum(jnp.where(before, listed[None, :], 0), axis=1)
    rank = jnp.where(listed > 0, ahead, count + local - ahead)
    place = rank[None, :] == local[:, None]
    order = jnp.sum(jnp.where(place, local[None, :], 0), axis=1)
    base = jnp.sum(jnp.where(place, held[None, :], 0), axis=1) * crows
    info = jnp.stack([count, my_y.astype(I32), my_col.astype(I32)])
    pieces = pieces + (hop(strip, core=1),)
    pieces = pieces + (hop(z_right, core=1), hop(z_left, core=1))
    z_low, z_high, order, base, info = lax.optimization_barrier((z_low, z_high, order, base, info))
    pieces = pieces + (hop(z_low, core=1), hop(z_high, core=1))

    *query_parts, label_own, label_a, label_b, label_c, label_d = score_and_grads(
        order,
        base,
        info,
        positives.reshape(-1, 128),
        (own, right, left, far_low, far_high),
        pieces,
    )
    label_hops = ring_open(label_b, label_c, shift)
    mine_u, mine_v, part_u, part_v = query_parts
    u = add(mine_u, hop(part_u, core=1))
    v = add(mine_v, hop(part_v, core=1))
    u_own, u_a, u_b, u_c, u_d = cut(u)
    v_own, v_a, v_b, v_c, v_d = cut(v)
    u_hops, v_hops = ring_open(u_b, u_c, along_x), ring_open(v_b, v_c, along_z)
    u_far, v_far = ring_far(u_a, u_d, *u_hops), ring_far(v_a, v_d, *v_hops)
    label_left, label_right, *_ = lax.optimization_barrier((*label_hops, *u_far, *v_far))
    u = add(*ring_close(u_own, u_far, *u_hops, along_x))
    v = add(*ring_close(v_own, v_far, *v_hops, along_z))
    label_sums = ring_far(label_a, label_d, label_left, label_right)
    label_parts = ring_close(label_own, label_sums, label_left, label_right, shift)
    u = ring_sum_small(u, along_z)
    v = ring_sum_small(v, along_x)
    query_grad = jnp.concatenate([u[0], v[0]]).astype(F32)

    flat = lambda value: value.reshape(n_col * quarter, width)
    new_codes, new_scales, new_master, new_first, new_second = update(
        *(flat(part) for part in label_parts),
        flat(label_master),
        flat(first_moment),
        flat(second_moment),
    )
    shape = label_master.shape
    return (
        query_grad[None],
        new_codes.reshape(shape),
        new_scales.reshape(n_col, quarter, width // BLK),
        new_master.reshape(shape),
        new_first.reshape(shape),
        new_second.reshape(shape),
    )


def solution(mesh):
    in_specs = (
        P("query", "cluster", None),
        P("query", None),
        P("query", "cluster"),
        P(),
        P("cluster", "query", None),
        P("cluster", "query", None),
        P("cluster", "query", None),
        P("cluster", "query", None),
        P("cluster", "query", None),
    )
    out_specs = (
        P("query", "cluster", None),
        P("cluster", "query", None),
        P("cluster", "query", None),
        P("cluster", "query", None),
        P("cluster", "query", None),
        P("cluster", "query", None),
    )

    return jax.shard_map(
        per_device, mesh=mesh, in_specs=in_specs, out_specs=out_specs, check_vma=False
    )
```
